256 devices in a mesh: ctx: 32 (over z, x), head: 8 (over y, core).
Axes of the slice: x: 4, y: 4, z: 8, core: 2. Of those that a mesh axis runs over, the one named last changes fastest.
Arguments:
- x_in: bfloat16 [8192, 16384], P('ctx', 'head'), may hold values from -6 to 6
- z_gate: bfloat16 [8192, 16384], P('ctx', 'head'), may hold values from -6 to 6
- step_size: float32 [256, 8192], P('head', 'ctx'), may hold values from 0.0005859375 to 2.24
- decay_rate: float32 [256], P('head'), may hold values from 0.0029296875 to 0.67
- conv_weight: bfloat16 [4, 16384], P(None, 'head'), may hold values from -3 to 3
- conv_bias: bfloat16 [16384], P('head'), may hold values from -3 to 3
- bc_proj: bfloat16 [32, 16384], P(None, 'head'), may hold values from -0.0234375 to 0.0234375
- skip_gain: float32 [256], P('head'), may hold values from 0.5 to 1.5
- queries: bfloat16 [8192, 8192], P('ctx', 'head'), may hold values from -156.42136 to 156.42136
- keys: bfloat16 [8192, 1024], P('ctx', 'head'), may hold values from -6 to 6
- values: bfloat16 [8192, 1024], P('ctx', 'head'), may hold values from -6 to 6
Outputs:
- mamba_out: bfloat16 [8192, 16384], P('ctx', 'head')
- attn_out: bfloat16 [8192, 8192], P('ctx', 'head')
The draws below stay inside these ranges and needn't reach their ends.
All inputs are finite; a program needn't handle non-finite values.
Results may differ from the reference program's by a relative error of at most 0.0055.
Values may be sent and summed in bfloat16 or wider, within the bound.
A program may use at most 64 MiB of HBM per device.

```python
import math
import jax
import jax.numpy as jnp
from jax import lax

DI = 16384
NS = 16
KW = 4
H = 64
KVH = 8
HD = 128
PM = 64
BLOCK = 256
TOKENS_PER_PART = 256
STATE_MIX_HEADS = 256
TOKEN_COUNT = 8192


def decay_pair(key):
    folded = jax.random.fold_in(key, 5)
    random_seeds = jax.random.split(folded, 7)
    share = 0.5
    slow_mask = jax.random.uniform(random_seeds[0], (STATE_MIX_HEADS,), jnp.float32) < share
    slow_total = jax.random.uniform(random_seeds[1], (STATE_MIX_HEADS,), jnp.float32, 1.0, 1.4) / TOKEN_COUNT
    fast_total = jnp.exp(jax.random.uniform(random_seeds[2], (STATE_MIX_HEADS,), jnp.float32, math.log(1.0 / 50.0), math.log(1.0 / 30.0)))
    base_step = jnp.where(slow_mask, 0.04, 0.05)
    decay_rate_list = jnp.where(slow_mask, slow_total, fast_total) / base_step
    block_factor = jnp.exp(jax.random.uniform(random_seeds[3], (STATE_MIX_HEADS, TOKEN_COUNT // TOKENS_PER_PART), jnp.float32, math.log(0.5), math.log(2.0)))
    coarse_multiplier = jnp.exp(jax.random.uniform(random_seeds[4], (STATE_MIX_HEADS, TOKEN_COUNT), jnp.float32, math.log(0.5), math.log(2.0)))
    step_size_list = base_step[:, None] * jnp.repeat(block_factor, TOKENS_PER_PART, axis=1) * coarse_multiplier
    starts = jax.random.randint(random_seeds[5], (2,), 0, TOKEN_COUNT - TOKENS_PER_PART + 1)
    positions = jnp.arange(TOKEN_COUNT, dtype=jnp.int32)
    within_bounds = (positions[None, :] >= starts[:, None]) & (positions[None, :] < starts[:, None] + TOKENS_PER_PART)
    spike_error = jax.random.uniform(random_seeds[6], (2, STATE_MIX_HEADS), jnp.float32, 0.22, 0.4)
    token_level = spike_error / (decay_rate_list[None, :] * TOKENS_PER_PART)
    spike_step_rows = jnp.sum(jnp.where(within_bounds[:, None, :], token_level[:, :, None], 0.0), axis=0) * coarse_multiplier
    has_spike_steps = jnp.any(within_bounds, axis=0)
    step_size_list = jnp.where(has_spike_steps[None, :], spike_step_rows, step_size_list)
    return (step_size_list, decay_rate_list)


def draw_step_size(key, part):
    step_size_list, decay_rate_list = decay_pair(key)
    return step_size_list.astype(jnp.float32)


def draw_decay_rate(key, part):
    step_size_list, decay_rate_list = decay_pair(key)
    return decay_rate_list.astype(jnp.float32)


def attention_pair(key):
    folded = jax.random.fold_in(key, 11)
    random_seeds = jax.random.split(folded, 2)
    key_base = jnp.clip(jax.random.normal(random_seeds[0], (TOKEN_COUNT, KVH, HD), jnp.float32), -6.0, 6.0)
    query_base = 2.5 * jnp.clip(jax.random.normal(random_seeds[1], (TOKEN_COUNT, H, HD), jnp.float32), -6.0, 6.0)
    return (query_base.reshape(TOKEN_COUNT, H * HD), key_base.reshape(TOKEN_COUNT, KVH * HD))


def draw_queries(key, part):
    query_base, key_base = attention_pair(key)
    return query_base.astype(jnp.bfloat16)


def draw_keys(key, part):
    query_base, key_base = attention_pair(key)
    return key_base.astype(jnp.bfloat16)


def level_of(own_key, shape, pieces, least, high):
    def one(dim, parts):
        steps = jax.random.uniform(jax.random.fold_in(jax.random.fold_in(own_key, 6), dim), (parts,), jnp.float32, least / len(pieces), high / len(pieces))
        return jnp.repeat(jnp.exp(steps), shape[dim] // parts).reshape((-1,) + (1,) * (len(shape) - dim - 1))

    loudness = one(*pieces[0])
    for cut in pieces[1:]:
        loudness = loudness * one(*cut)
    return loudness


def gaussian(stream_key, shape, spread, limit, pieces=(), held_as=jnp.bfloat16):
    values = spread * jax.random.normal(stream_key, shape, jnp.float32)
    if pieces:
        values = values * level_of(stream_key, shape, pieces, -0.22, 0.18)
    return jnp.clip(values, -limit, limit).astype(held_as)


def setup_inputs(seed: int = 0) -> dict:
    key_list = jax.random.split(jax.random.key(seed), 12)
    return {
        "x_in": gaussian(key_list[0], (TOKEN_COUNT, DI), 1.0, 6.0, ((0, 32), (1, 8))),
        "z_gate": gaussian(key_list[1], (TOKEN_COUNT, DI), 1.0, 6.0, ((0, 32), (1, 8))),
        "step_size": draw_step_size(jax.random.fold_in(key_list[11], 71), 0),
        "decay_rate": draw_decay_rate(jax.random.fold_in(key_list[11], 71), 0),
        "conv_weight": gaussian(key_list[4], (KW, DI), KW ** -0.5, 3.0, ((1, 8),)),
        "conv_bias": gaussian(key_list[5], (DI,), 0.5, 3.0, ((0, 8),)),
        "bc_proj": gaussian(key_list[6], (2 * NS, DI), (4 * DI) ** -0.5, 0.0234375, ((1, 8),)),
        "skip_gain": jnp.clip(0.5 + 1.0 * jax.random.uniform(key_list[7], (STATE_MIX_HEADS,), jnp.float32) ** level_of(key_list[7], (STATE_MIX_HEADS,), ((0, 8),), -0.2, 0.2), 0.5, 1.5),
        "queries": draw_queries(jax.random.fold_in(key_list[11], 71), 0),
        "keys": draw_keys(jax.random.fold_in(key_list[11], 71), 0),
        "values": gaussian(key_list[10], (TOKEN_COUNT, KVH * HD), 1.0, 6.0, ((0, 32), (1, 8))),
    }


def gated_conv(x_in, conv_weight, conv_bias, rim_rows):
    row_count = x_in.shape[0]
    padded = jnp.concatenate([rim_rows, x_in], axis=0)
    summed = jnp.broadcast_to(conv_bias.astype(jnp.float32)[None, :], x_in.shape)
    for offset in range(KW):
        summed = summed + padded[offset:offset + row_count].astype(jnp.float32) * conv_weight[offset].astype(jnp.float32)[None, :]
    return jax.nn.silu(summed).astype(jnp.bfloat16)

def block_terms(block_x, b_rows, c_rows, step_rows, decay_rows, skip_gain):
    length = block_x.shape[0]
    cumulative = jnp.cumsum(decay_rows, axis=1)
    later = lax.broadcasted_iota(jnp.int32, (length, length), 0) >= lax.broadcasted_iota(jnp.int32, (length, length), 1)
    gap_matrix = cumulative[:, :, None] - cumulative[:, None, :]
    decays = jnp.where(later[None], jnp.exp(jnp.minimum(gap_matrix, 0.0)), 0.0)
    scores = jnp.dot(c_rows.T, b_rows, precision=lax.Precision.HIGHEST, preferred_element_type=jnp.float32)
    mixing = (decays * scores[None] * step_rows[:, None, :]).astype(jnp.bfloat16)
    mixing = lax.optimization_barrier(mixing).astype(jnp.float32)
    wide_x = block_x.astype(jnp.float32)
    within_bounds = jnp.einsum('hts,shp->thp', mixing, wide_x)
    local_term = within_bounds + skip_gain[None, :, None] * wide_x
    tail_weight = jnp.exp(cumulative[:, -1:] - cumulative) * step_rows
    weighted = tail_weight[:, None, :] * b_rows[None]
    added_state = jnp.einsum('hns,shp->hpn', weighted, wide_x, precision=lax.Precision.HIGHEST)
    return (local_term, cumulative, added_state)

def mamba_mixer(x_in, z_gate, step_size, decay_rate, conv_weight, conv_bias, bc_proj, skip_gain):
    head_count = DI // PM
    x_conv = gated_conv(x_in, conv_weight, conv_bias, jnp.zeros((KW - 1, DI), jnp.bfloat16))
    summed_bc = jnp.dot(bc_proj, x_conv.T, preferred_element_type=jnp.float32)
    log_decay = -step_size * decay_rate[:, None]

    def advance(entering, block_number):
        first_row = block_number * BLOCK
        block_x = lax.dynamic_slice_in_dim(x_conv, first_row, BLOCK, 0).reshape(BLOCK, head_count, PM)
        b_rows = lax.dynamic_slice_in_dim(summed_bc[:NS], first_row, BLOCK, 1)
        c_rows = lax.dynamic_slice_in_dim(summed_bc[NS:], first_row, BLOCK, 1)
        step_rows = lax.dynamic_slice_in_dim(step_size, first_row, BLOCK, 1)
        decay_rows = lax.dynamic_slice_in_dim(log_decay, first_row, BLOCK, 1)
        local_term, cumulative, added_state = block_terms(block_x, b_rows, c_rows, step_rows, decay_rows, skip_gain)
        carried = jnp.einsum('nt,hpn->thp', c_rows, entering, precision=lax.Precision.HIGHEST) * jnp.exp(cumulative).T[:, :, None]
        gate_rows = lax.dynamic_slice_in_dim(z_gate, first_row, BLOCK, 0).astype(jnp.float32)
        result = ((local_term + carried).reshape(BLOCK, DI) * jax.nn.silu(gate_rows)).astype(jnp.bfloat16)
        leaving = jnp.exp(cumulative[:, -1])[:, None, None] * entering + added_state
        return (leaving, result)
    numbers = jnp.arange(TOKEN_COUNT // BLOCK, dtype=jnp.int32)
    _, results = lax.scan(advance, jnp.zeros((head_count, PM, NS), jnp.float32), numbers)
    return results.reshape(TOKEN_COUNT, DI)

def attention(queries, keys, values):
    group = H // KVH
    scale_factor = 1.0 / math.sqrt(HD)
    block_rows = math.gcd(TOKEN_COUNT, 128)
    key_heads = keys.reshape(TOKEN_COUNT, KVH, HD).astype(jnp.float32)
    value_heads = values.reshape(TOKEN_COUNT, KVH, HD).astype(jnp.float32)
    positions = jnp.arange(TOKEN_COUNT, dtype=jnp.int32)

    def one_block(block_number):
        first_row = block_number * block_rows
        query_rows = lax.dynamic_slice_in_dim(queries, first_row, block_rows, 0).reshape(block_rows, KVH, group, HD).astype(jnp.float32)
        scores = jnp.einsum('tkgd,skd->kgts', query_rows, key_heads) * scale_factor
        visible = (first_row + jnp.arange(block_rows, dtype=jnp.int32))[:, None] >= positions[None, :]
        scores = jnp.where(visible, scores, -1e+30)
        best_score = lax.optimization_barrier(jnp.max(scores, axis=-1, keepdims=True))
        exp_scores = jnp.where(visible, jnp.exp(scores - best_score), 0.0)
        mass_sum = lax.optimization_barrier(jnp.sum(exp_scores, axis=-1))
        weights = lax.optimization_barrier(exp_scores.astype(jnp.bfloat16)).astype(jnp.float32)
        mixed = jnp.einsum('kgts,skd->tkgd', weights, value_heads)
        normed = mixed / jnp.transpose(mass_sum, (2, 0, 1))[..., None]
        return normed.reshape(block_rows, H * HD).astype(jnp.bfloat16)
    results = lax.map(one_block, jnp.arange(TOKEN_COUNT // block_rows, dtype=jnp.int32))
    return results.reshape(TOKEN_COUNT, H * HD)

def reference(x_in, z_gate, step_size, decay_rate, conv_weight, conv_bias, bc_proj, skip_gain, queries, keys, values):
    mamba_out = mamba_mixer(x_in, z_gate, step_size, decay_rate, conv_weight, conv_bias, bc_proj, skip_gain)
    attn_out = attention(queries, keys, values)
    return (mamba_out, attn_out)
```

```python
import functools
import jax
import jax.numpy as jnp
from jax import lax
from jax.experimental import pallas as pl
from jax.experimental.pallas import tpu as pltpu
from jax.sharding import PartitionSpec as P

NS = 16
KW = 4
HD = 128
PM = 64
BLOCK = 256
NX = 4
MESH = pl.DeviceIdType.MESH
F32 = jnp.float32
BF16 = jnp.bfloat16
NEG = -1e30


def nt(a, b):
    return lax.dot_general(a, b, (((1,), (1,)), ((), ())), preferred_element_type=F32)


def tn(a, b):
    return lax.dot_general(a, b, (((0,), (0,)), ((), ())), preferred_element_type=F32)


def nn(a, b):
    return lax.dot_general(a, b, (((1,), (0,)), ((), ())), preferred_element_type=F32)


def parts2(a):
    high = a.astype(BF16)
    return high, (a - high.astype(F32)).astype(BF16)


def parts3(a):
    high = a.astype(BF16)
    rest = a - high.astype(F32)
    middle = rest.astype(BF16)
    return high, middle, (rest - middle.astype(F32)).astype(BF16)


def kernel(
    dims,
    x_hbm,
    z_hbm,
    step_ref,
    rate_ref,
    taps_ref,
    bias_ref,
    proj_ref,
    skip_ref,
    q_hbm,
    k_hbm,
    v_hbm,
    mo_hbm,
    ao_hbm,
    xv,
    zv,
    qv,
    kv,
    halo,
    padded,
    xc,
    mo,
    ao,
    qp,
    best,
    acc,
    part,
    rs_buf,
    ag_buf,
    ld,
    cum_ref,
    cumt_ref,
    st_buf,
    tl_buf,
    prow,
    tlp_ref,
    rfull,
    tlr_ref,
    zr_buf,
    ztl_buf,
    ebuf,
    loc,
    halo_s,
    halo_r,
    kz_s,
    kz_r,
    fl_s,
    fl_r,
    fr_s,
    fr_r,
    op_s,
    op_r,
    rs_s,
    rs_r,
    ag_s,
    ag_r,
    s1_s,
    s1_r,
    t1_s,
    t1_r,
    s2_s,
    s2_r,
    t2_s,
    t2_r,
    s3_s,
    s3_r,
):
    nz, nh = dims
    nctx = nz * NX
    rows, channels = xv.shape
    heads = step_ref.shape[0]
    pairs = channels // 128
    quarter = channels // NX
    qheads = qp.shape[0]
    ci = lax.axis_index("ctx")
    hi = lax.axis_index("head")
    cz = lax.div(ci, NX)
    cx = lax.rem(ci, NX)

    def at_z(z):
        return {"ctx": z * NX + cx}

    def at_x(x):
        return {"ctx": cz * NX + x}

    def turned(x):
        return lax.rem(x + 2 * NX, NX)

    def local(src, dst, number):
        return pltpu.make_async_copy(src, dst, loc.at[number])

    own = pl.ds(pl.multiple_of(ci * rows, rows), rows)
    copies = [
        local(k_hbm, kv.at[0, own], 0),
        local(v_hbm, kv.at[1, own], 1),
        local(x_hbm, xv, 2),
        local(q_hbm, qv, 3),
        local(z_hbm, zv, 4),
    ]
    for copy in copies:
        copy.start()

    barrier = pltpu.get_barrier_semaphore()

    def greet(device):
        pl.semaphore_signal(barrier, inc=1, device_id=device, device_id_type=MESH)

    for d in range(1, nh):
        greet({"head": lax.rem(hi + d, nh)})
    for d in range(1, NX):
        greet(at_x(lax.rem(cx + d, NX)))
    for d in range(1, nz):
        greet(at_z(lax.rem(cz + d, nz)))
    greet({"ctx": lax.rem(ci + 1, nctx)})
    greet({"ctx": lax.rem(ci + nctx - 1, nctx)})
    pl.semaphore_wait(barrier, nh + NX + nz - 1)

    def remote(src, dst, send, recv, device):
        return pltpu.make_async_remote_copy(
            src_ref=src,
            dst_ref=dst,
            send_sem=send,
            recv_sem=recv,
            device_id=device,
            device_id_type=MESH,
        )

    def halo_copy():
        return remote(
            x_hbm.at[pl.ds(rows - 16, 16)],
            halo,
            halo_s.at[0],
            halo_r.at[0],
            {"ctx": lax.rem(ci + 1, nctx)},
        )

    @pl.when(ci < nctx - 1)
    def _():
        halo_copy().start()

    def block(r, x):
        return kv.at[:, pl.ds(pl.multiple_of((r * NX + x) * rows, rows), rows), :]

    def z_copy(r):
        return remote(
            block(r, cx), block(r, cx), kz_s.at[r], kz_r.at[r], at_z(lax.rem(cz + 1, nz))
        )

    def right_copy(r):
        return remote(
            block(r, cx), block(r, cx), fl_s.at[r], fl_r.at[r], at_x(turned(cx + 1))
        )

    def left_copy(r):
        return remote(
            block(r, cx), block(r, cx), fr_s.at[r], fr_r.at[r], at_x(turned(cx - 1))
        )

    def far_copy(r):
        way = 1 - 2 * lax.rem(r, 2)
        moved = block(r, turned(cx - way))
        return remote(moved, moved, op_s.at[r], op_r.at[r], at_x(turned(cx + way)))

    def stage_a(t):
        r = cz - t

        @pl.when(r >= 0)
        def _():
            @pl.when(r < cz)
            def _():
                z_copy(jnp.maximum(r, 0)).wait_recv()

            @pl.when(cz < nz - 1)
            def _():
                z_copy(jnp.maximum(r, 0)).start()

            right_copy(jnp.maximum(r, 0)).start()
            left_copy(jnp.maximum(r, 0)).start()

    def stage_b(t):
        r = cz - t

        @pl.when(r >= 0)
        def _():
            safe = jnp.maximum(r, 0)
            right_copy(safe).wait_recv()
            left_copy(safe).wait_recv()
            far_copy(safe).start()

    def stage_c(t):
        r = cz - t

        @pl.when(r >= 0)
        def _():
            far_copy(jnp.maximum(r, 0)).wait_recv()

    copies[0].wait()
    copies[1].wait()
    stage_a(0)

    copies[2].wait()

    @pl.when(ci > 0)
    def _():
        halo_copy().wait_recv()

    @pl.when(ci == 0)
    def _():
        halo[...] = jnp.zeros_like(halo)

    width = padded.shape[1]

    @pl.loop(0, channels // width)
    def _(piece):
        columns = pl.ds(pl.multiple_of(piece * width, width), width)
        padded[0:16, :] = halo[:, columns].astype(F32)
        padded[16 : 16 + rows, :] = xv[:, columns].astype(F32)
        summed = jnp.broadcast_to(bias_ref[:, columns].astype(F32), (rows, width))
        for offset in range(KW):
            summed = (
                summed
                + padded[16 - KW + 1 + offset : 16 - KW + 1 + offset + rows, :]
                * taps_ref[offset : offset + 1, columns].astype(F32)
            )
        xc[:, columns] = (summed * jax.nn.sigmoid(summed)).astype(BF16)

    partial = nt(proj_ref[...], xc[...])
    for p in range(8):
        part[p] = partial[8 * (p // 2) : 8 * (p // 2) + 8, 128 * (p % 2) : 128 * (p % 2) + 128]

    def rs_copy(d):
        peer = lax.rem(hi + d, nh)
        return remote(
            part.at[peer], rs_buf.at[hi], rs_s.at[d], rs_r.at[d], {"head": peer}
        )

    def ag_copy(d):
        peer = lax.rem(hi + d, nh)
        return remote(
            ag_buf.at[hi], ag_buf.at[hi], ag_s.at[d], ag_r.at[d], {"head": peer}
        )

    for d in range(1, nh):
        rs_copy(d).start()
    rs_buf[hi] = part[hi]

    stage_a(1)
    stage_b(0)

    for h in range(heads):
        ld[h : h + 1, :] = step_ref[h : h + 1, :] * (-rate_ref[h])
    first = lax.broadcasted_iota(jnp.int32, (rows, rows), 0)
    second = lax.broadcasted_iota(jnp.int32, (rows, rows), 1)
    upper = (first <= second).astype(F32).astype(BF16)
    lower = (first >= second).astype(F32).astype(BF16)
    pieces = parts3(ld[...])
    cum = nn(pieces[0], upper) + (nn(pieces[1], upper) + nn(pieces[2], upper))
    cum_ref[...] = cum
    cumt_ref[...] = nt(lower, pieces[0]) + (nt(lower, pieces[1]) + nt(lower, pieces[2]))
    tl_buf[cx] = jnp.broadcast_to(cum[:, rows - 1 : rows], (heads, 128))

    copies[3].wait()
    factor = (HD**-0.5) * 1.4426950408889634
    for h in range(qheads):
        high, low = parts2(qv[:, HD * h : HD * h + HD].astype(F32) * factor)
        qp[h, :, :HD] = high
        qp[h, :, HD:] = low

    for d in range(1, nh):
        rs_copy(d).wait_recv()
    total = rs_buf[0]
    for p in range(1, nh):
        total = total + rs_buf[p]
    ag_buf[hi] = total
    for d in range(1, nh):
        ag_copy(d).start()

    stage_a(2)
    stage_b(1)
    stage_c(0)

    span = NX * rows

    def attend(r, masked):
        keys = kv[0, pl.ds(pl.multiple_of(r * span, span), span), :]
        values = kv[1, pl.ds(pl.multiple_of(r * span, span), span), :]
        keys2 = jnp.concatenate([keys, keys], axis=1)
        values2 = jnp.concatenate([values, jnp.ones((span, HD), BF16)], axis=1)

        @pl.loop(0, qheads)
        def _(h):
            s = nt(qp[h], keys2)
            if masked:
                token = cx * rows + lax.broadcasted_iota(jnp.int32, (rows, span), 0)
                position = lax.broadcasted_iota(jnp.int32, (rows, span), 1)
                s = jnp.where(token >= position, s, NEG)
            top = jnp.max(s, axis=1, keepdims=True)
            if masked:
                new = jnp.broadcast_to(top, (rows, 128))
            else:
                old = best[h]
                new = jnp.maximum(old, top)
            weights = jnp.concatenate(
                [
                    jnp.exp2(s[:, 128 * j : 128 * j + 128] - new).astype(BF16)
                    for j in range(span // 128)
                ],
                axis=1,
            )
            product = nn(weights, values2)
            if masked:
                acc[h] = product
            else:
                shrink = jnp.exp2(old - new)
                acc[h] = acc[h] * jnp.concatenate([shrink, shrink], axis=1) + product
            best[h] = new

    attend(cz, True)

    def attend_step(t):
        @pl.when(cz >= t)
        def _():
            attend(jnp.maximum(cz - t, 0), False)

    for d in range(1, nh):
        ag_copy(d).wait_recv()

    def vector_rows(first_group):
        return jnp.concatenate(
            [
                jnp.concatenate([ag_buf[2 * g], ag_buf[2 * g + 1]], axis=1)
                for g in (first_group, first_group + 1)
            ],
            axis=0,
        )

    def x_peer_copies(d):
        peer = lax.rem(cx + d, NX)
        return (
            remote(st_buf.at[cx], st_buf.at[cx], s1_s.at[d], s1_r.at[d], at_x(peer)),
            remote(tl_buf.at[cx], tl_buf.at[cx], t1_s.at[d], t1_r.at[d], at_x(peer)),
        )

    def lane_pick(a, b):
        lane = lax.broadcasted_iota(jnp.int32, a.shape, 1)
        return jnp.where(lane < PM, a, b)

    def added_state():
        b_rows = vector_rows(0)
        cum = cum_ref[...]
        tail = jnp.exp(cum[:, rows - 1 : rows] - cum) * step_ref[...]
        for k in range(pairs):
            weighted = jnp.concatenate(
                [tail[2 * k : 2 * k + 1] * b_rows, tail[2 * k + 1 : 2 * k + 2] * b_rows],
                axis=0,
            )
            high, low = parts2(weighted)
            out = nn(jnp.concatenate([high, low], axis=0), xc[:, 128 * k : 128 * k + 128])
            out = out[: 2 * NS] + out[2 * NS :]
            st_buf[cx, :, 128 * k : 128 * k + 128] = lane_pick(out[:NS], out[NS:]).astype(BF16)
        for d in range(1, NX):
            for copy in x_peer_copies(d):
                copy.start()

    def pair_row(logs, k):
        return lane_pick(logs[2 * k : 2 * k + 1], logs[2 * k + 1 : 2 * k + 2])

    def z_peer_copies(d):
        target = lax.rem(cz + d, nz)
        columns = pl.ds(pl.multiple_of(cx * quarter, quarter), quarter)
        return (
            remote(rfull.at[:, columns], zr_buf.at[cz], s2_s.at[d], s2_r.at[d], at_z(target)),
            remote(tlr_ref, ztl_buf.at[cz], t2_s.at[d], t2_r.at[d], at_z(target)),
        )

    def row_state():
        for d in range(1, NX):
            for copy in x_peer_copies(d):
                copy.wait_recv()
        logs = [tl_buf[x] for x in range(NX)]
        before = jnp.zeros_like(logs[0])
        whole = jnp.zeros_like(logs[0])
        for x in range(NX):
            before = jnp.where(x == cx, whole, before)
            whole = whole + logs[x]
        tlp_ref[...] = before
        tlr_ref[...] = whole
        shrinks = [jnp.exp(a) for a in logs]
        for k in range(pairs):
            columns = slice(128 * k, 128 * k + 128)
            running = jnp.zeros((NS, 128), F32)
            mine = jnp.zeros((NS, 128), F32)
            for x in range(NX):
                mine = jnp.where(x == cx, running, mine)
                running = running * pair_row(shrinks[x], k) + st_buf[x, :, columns].astype(F32)
            prow[:, columns] = mine
            rfull[:, columns] = running
        for d in range(1, nz):

            @pl.when(cz + d < nz)
            def _(d=d):
                for copy in z_peer_copies(d):
                    copy.start()

    def e_copy(d):
        peer = lax.rem(cx + d, NX)
        columns = pl.ds(pl.multiple_of(cx * quarter, quarter), quarter)
        return remote(
            ebuf.at[:, columns], ebuf.at[:, columns], s3_s.at[d], s3_r.at[d], at_x(peer)
        )

    def e_arrival(d):
        peer = lax.rem(cx + NX - d, NX)
        columns = pl.ds(pl.multiple_of(peer * quarter, quarter), quarter)
        return remote(
            ebuf.at[:, columns], ebuf.at[:, columns], s3_s.at[d], s3_r.at[d], at_x(peer)
        )

    def entering_rows():
        columns = pl.ds(pl.multiple_of(cx * quarter, quarter), quarter)
        ebuf[:, columns] = jnp.zeros((NS, quarter), F32)
        for d in range(1, nz):

            @pl.when(cz >= d)
            def _(d=d):
                for copy in z_peer_copies(d):
                    copy.wait_recv()

        @pl.loop(0, cz)
        def _(z):
            shrink = jnp.exp(ztl_buf[z, pl.ds(pl.multiple_of(cx * 8, 8), 8), :])
            spread = jnp.concatenate([pair_row(shrink, k) for k in range(quarter // 128)], axis=1)
            ebuf[:, columns] = ebuf[:, columns] * spread + zr_buf[z]

        for d in range(1, NX):
            e_copy(d).start()

    def finish():
        for d in range(1, NX):
            e_arrival(d).wait_recv()
        copies[4].wait()
        b_rows = vector_rows(0)
        c_rows = vector_rows(2)
        b_high, b_low = parts2(b_rows)
        c_high, c_low = parts2(c_rows)
        c3 = jnp.concatenate([c_high, c_low, c_high], axis=0)
        scores = tn(c3, jnp.concatenate([b_high, b_high, b_low], axis=0))
        first = lax.broadcasted_iota(jnp.int32, (rows, rows), 0)
        second = lax.broadcasted_iota(jnp.int32, (rows, rows), 1)
        scores = jnp.where(first >= second, scores, 0.0)
        reach = jnp.exp(tlp_ref[...])
        for k in range(pairs):
            columns = slice(128 * k, 128 * k + 128)
            here = xc[:, columns]
            local_terms = []
            far_decays = []
            for h in (2 * k, 2 * k + 1):
                level = cumt_ref[:, h : h + 1]
                gap = level - cum_ref[h : h + 1, :]
                mixing = jnp.exp(jnp.minimum(gap, 0.0)) * scores * step_ref[h : h + 1, :]
                local_terms.append(nn(mixing.astype(BF16), here))
                far_decays.append(jnp.broadcast_to(jnp.exp(level), (rows, 128)))
            entering = ebuf[:, columns] * pair_row(reach, k) + prow[:, columns]
            e_high, e_low = parts2(entering)
            carried = tn(c3, jnp.concatenate([e_high, e_high, e_low], axis=0))
            lane = lax.broadcasted_iota(jnp.int32, (rows, 128), 1) < PM
            gain = jnp.where(lane, skip_ref[2 * k], skip_ref[2 * k + 1])
            y = (
                jnp.where(lane, local_terms[0], local_terms[1])
                + carried * jnp.where(lane, far_decays[0], far_decays[1])
                + gain * here.astype(F32)
            )
            gate = zv[:, columns].astype(F32)
            mo[:, columns] = (y * (gate * jax.nn.sigmoid(gate))).astype(BF16)

    added_state()

    @pl.loop(1, nz)
    def _(t):
        stage_a(t + 2)
        stage_b(t + 1)
        stage_c(t)
        attend_step(t)

        @pl.when(t == 1)
        def _():
            row_state()

        @pl.when(t == 2)
        def _():
            entering_rows()

    finish()
    write_mo = local(mo, mo_hbm, 5)
    write_mo.start()
    for h in range(qheads):
        ao[:, HD * h : HD * h + HD] = (acc[h, :, :HD] / acc[h, :, HD:]).astype(BF16)
    write_ao = local(ao, ao_hbm, 6)
    write_ao.start()

    @pl.when(ci < nctx - 1)
    def _():
        halo_copy().wait_send()

    @pl.loop(0, cz + 1)
    def _(r):
        @pl.when(cz < nz - 1)
        def _():
            z_copy(r).wait_send()

        right_copy(r).wait_send()
        left_copy(r).wait_send()
        far_copy(r).wait_send()

    for d in range(1, nh):
        rs_copy(d).wait_send()
        ag_copy(d).wait_send()
    for d in range(1, NX):
        for copy in x_peer_copies(d):
            copy.wait_send()
        e_copy(d).wait_send()
    for d in range(1, nz):

        @pl.when(cz + d < nz)
        def _(d=d):
            for copy in z_peer_copies(d):
                copy.wait_send()

    write_mo.wait()
    write_ao.wait()


def body(
    dims,
    x_in,
    z_gate,
    step_size,
    decay_rate,
    conv_weight,
    conv_bias,
    bc_proj,
    skip_gain,
    queries,
    keys,
    values,
):
    nz, nh = dims
    rows, channels = x_in.shape
    heads = step_size.shape[0]
    qheads = queries.shape[1] // HD
    span = NX * nz * rows
    quarter = channels // NX
    dma = pltpu.SemaphoreType.DMA
    vmem = pl.BlockSpec(memory_space=pltpu.VMEM)
    smem = pl.BlockSpec(memory_space=pltpu.SMEM)
    hbm = pl.BlockSpec(memory_space=pl.ANY)
    v = pltpu.VMEM
    scratch = [
        v((rows, channels), BF16),
        v((rows, channels), BF16),
        v((rows, qheads * HD), BF16),
        v((2, span, HD), BF16),
        v((16, channels), BF16),
        v((16 + rows, 256), F32),
        v((rows, channels), BF16),
        v((rows, channels), BF16),
        v((rows, qheads * HD), BF16),
        v((qheads, rows, 2 * HD), BF16),
        v((qheads, rows, 128), F32),
        v((qheads, rows, 2 * HD), F32),
        v((8, 8, 128), F32),
        v((8, 8, 128), F32),
        v((8, 8, 128), F32),
        v((heads, rows), F32),
        v((heads, rows), F32),
        v((rows, heads), F32),
        v((NX, NS, channels), BF16),
        v((NX, heads, 128), F32),
        v((NS, channels), F32),
        v((heads, 128), F32),
        v((NS, channels), F32),
        v((heads, 128), F32),
        v((nz, NS, quarter), F32),
        v((nz, heads, 128), F32),
        v((NS, channels), F32),
        dma((7,)),
        dma((1,)),
        dma((1,)),
        *[dma((nz,)) for _ in range(8)],
        *[dma((nh,)) for _ in range(4)],
        *[dma((NX,)) for _ in range(4)],
        *[dma((nz,)) for _ in range(4)],
        *[dma((NX,)) for _ in range(2)],
    ]
    return pl.pallas_call(
        functools.partial(kernel, dims),
        out_shape=(
            jax.ShapeDtypeStruct((rows, channels), BF16),
            jax.ShapeDtypeStruct((rows, qheads * HD), BF16),
        ),
        in_specs=[hbm, hbm, vmem, smem, vmem, vmem, vmem, smem, hbm, hbm, hbm],
        out_specs=(hbm, hbm),
        scratch_shapes=scratch,
        compiler_params=pltpu.CompilerParams(
            collective_id=0, has_side_effects=True, vmem_limit_bytes=48 << 20
        ),
    )(
        x_in,
        z_gate,
        step_size,
        decay_rate,
        conv_weight,
        conv_bias.reshape(1, channels),
        bc_proj,
        skip_gain,
        queries,
        keys,
        values,
    )


def solution(mesh):
    dims = (mesh.shape["ctx"] // NX, mesh.shape["head"])
    return jax.shard_map(
        functools.partial(body, dims),
        mesh=mesh,
        in_specs=(
            P("ctx", "head"),
            P("ctx", "head"),
            P("head", "ctx"),
            P("head"),
            P(None, "head"),
            P("head"),
            P(None, "head"),
            P("head"),
            P("ctx", "head"),
            P("ctx", "head"),
            P("ctx", "head"),
        ),
        out_specs=(P("ctx", "head"), P("ctx", "head")),
        check_vma=False,
    )
```

```python
import functools
import jax
import jax.numpy as jnp
from jax import lax
from jax.experimental import pallas as pl
from jax.experimental.pallas import tpu as pltpu
from jax.sharding import PartitionSpec as P

NS = 16
KW = 4
HD = 128
PM = 64
BLOCK = 256
NX = 4
FORWARD = 4
MESH = pl.DeviceIdType.MESH
F32 = jnp.float32
BF16 = jnp.bfloat16
NEG = -1e30


def nt(a, b):
    return lax.dot_general(a, b, (((1,), (1,)), ((), ())), preferred_element_type=F32)


def tn(a, b):
    return lax.dot_general(a, b, (((0,), (0,)), ((), ())), preferred_element_type=F32)


def nn(a, b):
    return lax.dot_general(a, b, (((1,), (0,)), ((), ())), preferred_element_type=F32)


def parts2(a):
    high = a.astype(BF16)
    return high, (a - high.astype(F32)).astype(BF16)


def parts3(a):
    high = a.astype(BF16)
    rest = a - high.astype(F32)
    middle = rest.astype(BF16)
    return high, middle, (rest - middle.astype(F32)).astype(BF16)


def kernel(
    dims,
    x_hbm,
    z_hbm,
    step_hbm,
    rate_ref,
    taps_hbm,
    bias_hbm,
    proj_hbm,
    skip_ref,
    q_hbm,
    k_hbm,
    v_hbm,
    mo,
    ao,
    xv,
    zv,
    qv,
    kv,
    step_ref,
    taps_ref,
    bias_ref,
    proj_ref,
    halo,
    padded,
    xc,
    qp,
    best,
    acc,
    part,
    rs_buf,
    ag_buf,
    ld,
    cum_ref,
    cumt_ref,
    st_own,
    tl_own,
    st_buf,
    tl_buf,
    prefix,
    rq,
    tlr,
    zr_buf,
    ztl_buf,
    eq,
    ent_own,
    ent,
    loc,
    halo_s,
    halo_r,
    of_s,
    ob_s,
    o_r,
    ff_s,
    fb_s,
    f_r,
    fl_s,
    fl_r,
    fr_s,
    fr_r,
    half_s,
    half_r,
    rs_s,
    rs_r,
    ag_s,
    ag_r,
    s1_s,
    s1_r,
    t1_s,
    t1_r,
    s2_s,
    s2_r,
    t2_s,
    t2_r,
    s3_s,
    s3_r,
):
    nz, nh = dims
    rows, channels = xv.shape
    heads = step_ref.shape[0]
    pairs = channels // 128
    quarter = channels // NX
    qpairs = quarter // 128
    qheads = qp.shape[0]
    ci = lax.axis_index("ctx")
    hi = lax.axis_index("head")
    cz = lax.div(ci, NX)
    cx = lax.rem(ci, NX)
    nctx = nz * NX

    def at_z(z):
        return {"ctx": z * NX + cx}

    def at_x(x):
        return {"ctx": cz * NX + x}

    def turned(x):
        return lax.rem(x + 2 * NX, NX)

    def local(src, dst, number):
        return pltpu.make_async_copy(src, dst, loc.at[number])

    own = pl.ds(pl.multiple_of(ci * rows, rows), rows)
    load_k = local(k_hbm, kv.at[0, own], 0)
    load_v = local(v_hbm, kv.at[1, own], 1)
    load_q = local(q_hbm, qv, 2)
    load_x = local(x_hbm, xv, 3)
    load_z = local(z_hbm, zv, 4)
    small = [
        local(step_hbm, step_ref, 5),
        local(taps_hbm, taps_ref, 6),
        local(bias_hbm, bias_ref, 7),
        local(proj_hbm, proj_ref, 8),
    ]
    for copy in [load_k, load_v, load_q, *small, load_x, load_z]:
        copy.start()

    barrier = pltpu.get_barrier_semaphore()

    def greet(device):
        pl.semaphore_signal(barrier, inc=1, device_id=device, device_id_type=MESH)

    for d in range(1, nh):
        greet({"head": lax.rem(hi + d, nh)})
    for d in range(1, NX):
        greet(at_x(lax.rem(cx + d, NX)))
    for d in range(1, nz):
        greet(at_z(lax.rem(cz + d, nz)))
    greet({"ctx": lax.rem(ci + 1, nctx)})
    greet({"ctx": lax.rem(ci + nctx - 1, nctx)})

    load_q.wait()
    factor = (HD**-0.5) * 1.4426950408889634
    for h in range(qheads):
        high, low = parts2(qv[:, HD * h : HD * h + HD].astype(F32) * factor)
        qp[h, :, :HD] = high
        qp[h, :, HD:] = low
    load_k.wait()
    load_v.wait()
    for copy in small:
        copy.wait()

    pl.semaphore_wait(barrier, nh + NX + nz - 1)

    def remote(src, dst, send, recv, device):
        return pltpu.make_async_remote_copy(
            src_ref=src,
            dst_ref=dst,
            send_sem=send,
            recv_sem=recv,
            device_id=device,
            device_id_type=MESH,
        )

    def halo_copy():
        return remote(
            x_hbm.at[pl.ds(rows - 16, 16)],
            halo,
            halo_s.at[0],
            halo_r.at[0],
            {"ctx": lax.rem(ci + 1, nctx)},
        )

    @pl.when(ci < nctx - 1)
    def _():
        halo_copy().start()

    def place(r, x):
        return pl.ds(pl.multiple_of((r * NX + x) * rows, rows), rows)

    def moved(r, x, send, recv, device):
        block = kv.at[:, place(r, x), :]
        return remote(block, block, send, recv, device)

    opposite = turned(cx + 2)
    up = at_z(lax.rem(cz + 1, nz))
    down = at_z(lax.rem(cz + nz - 1, nz))

    def own_up(r):
        return moved(r, cx, of_s.at[r], o_r.at[r], up)

    def own_down(r):
        return moved(r, cx, ob_s.at[r], o_r.at[r], down)

    def far_up(r):
        return moved(r, opposite, ff_s.at[r], f_r.at[r], up)

    def far_down(r):
        return moved(r, opposite, fb_s.at[r], f_r.at[r], down)

    def to_right(r):
        return moved(r, cx, fl_s.at[r], fl_r.at[r], at_x(turned(cx + 1)))

    def to_left(r):
        return moved(r, cx, fr_s.at[r], fr_r.at[r], at_x(turned(cx - 1)))

    def half_copy(which):
        source, target = ((cx - 1, cx + 1), (cx + 1, cx - 1))[which]
        block = kv.at[which, place(cz, turned(source)), :]
        return remote(
            block, block, half_s.at[which], half_r.at[which], at_x(turned(target))
        )

    def hops_down(r):
        return lax.rem(r - cz + nz, nz)

    def goes_up(r):
        return (cz < nz - 1) & (cz - r >= 0) & (cz - r < FORWARD)

    def goes_down(r):
        return (r < nz - 1 - FORWARD) & (hops_down(r) < nz - 1 - FORWARD)

    def send_own(r, sideways):
        @pl.when(goes_up(r))
        def _():
            own_up(r).start()

        @pl.when(goes_down(r))
        def _():
            own_down(r).start()

        @pl.when(sideways)
        def _():
            to_right(r).start()
            to_left(r).start()

    def send_far(r):
        @pl.when(goes_up(r))
        def _():
            far_up(r).start()

        @pl.when(goes_down(r))
        def _():
            far_down(r).start()

    def row_up(t):
        return cz - t, (cz - t >= 0) & (t <= FORWARD)

    def row_down(t):
        r = lax.rem(cz + t, nz)
        return r, (r < nz - 1 - FORWARD) & (t <= nz - 1 - FORWARD)

    def own_events(t):
        for r, real in (row_up(t), row_down(t)):

            @pl.when(real)
            def _(r=r):
                safe = jnp.maximum(r, 0)
                own_up(safe).wait_recv()
                send_own(safe, safe < cz)

    def far_events(t):
        for r, real in (row_up(t), row_down(t)):

            @pl.when(real)
            def _(r=r):
                safe = jnp.maximum(r, 0)
                far_up(safe).wait_recv()
                send_far(safe)

    def side_events(t):
        for r, real in (row_up(t), row_down(t)):

            @pl.when(real & (r < cz))
            def _(r=r):
                safe = jnp.maximum(r, 0)
                to_right(safe).wait_recv()
                to_left(safe).wait_recv()

    send_own(cz, True)

    for h in range(heads):
        ld[h : h + 1, :] = step_ref[h : h + 1, :] * (-rate_ref[h])
    first = lax.broadcasted_iota(jnp.int32, (rows, rows), 0)
    second = lax.broadcasted_iota(jnp.int32, (rows, rows), 1)
    upper = (first <= second).astype(F32).astype(BF16)
    lower = (first >= second).astype(F32).astype(BF16)
    pieces = parts3(ld[...])
    cum = nn(pieces[0], upper) + (nn(pieces[1], upper) + nn(pieces[2], upper))
    cum_ref[...] = cum
    cumt_ref[...] = nt(lower, pieces[0]) + (nt(lower, pieces[1]) + nt(lower, pieces[2]))
    tl_own[...] = jnp.broadcast_to(cum[:, rows - 1 : rows], (heads, 128))

    def attend(start, span, opening):
        keys = kv[0, pl.ds(pl.multiple_of(start, rows), span), :]
        values = kv[1, pl.ds(pl.multiple_of(start, rows), span), :]
        keys2 = jnp.concatenate([keys, keys], axis=1)
        values2 = jnp.concatenate([values, jnp.ones((span, HD), BF16)], axis=1)

        unroll = 8 if span == rows else 4

        @pl.loop(0, qheads // unroll)
        def _(g):
            group = [g * unroll + u for u in range(unroll)]
            for h, s in [(h, nt(qp[h], keys2)) for h in group]:
                if opening:
                    token = lax.broadcasted_iota(jnp.int32, (rows, span), 0)
                    position = lax.broadcasted_iota(jnp.int32, (rows, span), 1)
                    s = jnp.where(token >= position, s, NEG)
                top = jnp.max(s, axis=1, keepdims=True)
                if opening:
                    new = jnp.broadcast_to(top, (rows, 128))
                else:
                    old = best[h]
                    new = jnp.maximum(old, top)
                weights = jnp.concatenate(
                    [
                        jnp.exp2(s[:, 128 * j : 128 * j + 128] - new).astype(BF16)
                        for j in range(span // 128)
                    ],
                    axis=1,
                )
                product = nn(weights, values2)
                if opening:
                    acc[h] = product
                else:
                    shrink = jnp.exp2(old - new)
                    acc[h] = acc[h] * jnp.concatenate([shrink, shrink], axis=1) + product
                best[h] = new

    load_x.wait()

    @pl.when(ci > 0)
    def _():
        halo_copy().wait_recv()

    @pl.when(ci == 0)
    def _():
        halo[...] = jnp.zeros_like(halo)

    width = padded.shape[1]

    @pl.loop(0, channels // width)
    def _(piece):
        columns = pl.ds(pl.multiple_of(piece * width, width), width)
        padded[0:16, :] = halo[:, columns].astype(F32)
        padded[16 : 16 + rows, :] = xv[:, columns].astype(F32)
        summed = jnp.broadcast_to(bias_ref[:, columns].astype(F32), (rows, width))
        for offset in range(KW):
            summed = (
                summed
                + padded[16 - KW + 1 + offset : 16 - KW + 1 + offset + rows, :]
                * taps_ref[offset : offset + 1, columns].astype(F32)
            )
        xc[:, columns] = (summed * jax.nn.sigmoid(summed)).astype(BF16)

    partial = nt(proj_ref[...], xc[...])
    for p in range(8):
        part[p] = partial[8 * (p // 2) : 8 * (p // 2) + 8, 128 * (p % 2) : 128 * (p % 2) + 128]

    def rs_copy(d):
        peer = lax.rem(hi + d, nh)
        return remote(
            part.at[peer], rs_buf.at[hi], rs_s.at[d], rs_r.at[d], {"head": peer}
        )

    def ag_copy(d):
        peer = lax.rem(hi + d, nh)
        return remote(
            ag_buf.at[hi], ag_buf.at[hi], ag_s.at[d], ag_r.at[d], {"head": peer}
        )

    for d in range(1, nh):
        rs_copy(d).start()
    rs_buf[hi] = part[hi]

    to_right(cz).wait_recv()
    to_left(cz).wait_recv()
    for which in range(2):
        half_copy(which).start()
    own_events(1)
    attend(ci * rows, rows, True)

    for d in range(1, nh):
        rs_copy(d).wait_recv()
    total = rs_buf[0]
    for p in range(1, nh):
        total = total + rs_buf[p]
    ag_buf[hi] = total
    for d in range(1, nh):
        ag_copy(d).start()

    for which in range(2):
        half_copy(which).wait_recv()
    send_far(cz)

    @pl.loop(0, cx)
    def _(x):
        attend((cz * NX + x) * rows, rows, False)

    for d in range(1, nh):
        ag_copy(d).wait_recv()

    def vector_rows(first_group):
        return jnp.concatenate(
            [
                jnp.concatenate([ag_buf[2 * g], ag_buf[2 * g + 1]], axis=1)
                for g in (first_group, first_group + 1)
            ],
            axis=0,
        )

    def lane_pick(a, b):
        lane = lax.broadcasted_iota(jnp.int32, a.shape, 1)
        return jnp.where(lane < PM, a, b)

    def pair_row(logs, k):
        return lane_pick(logs[2 * k : 2 * k + 1], logs[2 * k + 1 : 2 * k + 2])

    eight = 2 * qpairs

    def x_peer_copies(d):
        peer = lax.rem(cx + d, NX)
        its = pl.ds(pl.multiple_of(peer * eight, eight), eight)
        return (
            remote(st_own.at[peer], st_buf.at[cx], s1_s.at[d], s1_r.at[d], at_x(peer)),
            remote(tl_own.at[its], tl_buf.at[cx], t1_s.at[d], t1_r.at[d], at_x(peer)),
        )

    def added_state():
        b_rows = vector_rows(0)
        cum = cum_ref[...]
        tail = jnp.exp(cum[:, rows - 1 : rows] - cum) * step_ref[...]
        for k in range(pairs):
            weighted = jnp.concatenate(
                [tail[2 * k : 2 * k + 1] * b_rows, tail[2 * k + 1 : 2 * k + 2] * b_rows],
                axis=0,
            )
            high, low = parts2(weighted)
            out = nn(jnp.concatenate([high, low], axis=0), xc[:, 128 * k : 128 * k + 128])
            out = out[: 2 * NS] + out[2 * NS :]
            into = slice(128 * (k % qpairs), 128 * (k % qpairs) + 128)
            st_own[k // qpairs, :, into] = lane_pick(out[:NS], out[NS:]).astype(BF16)
        for d in range(1, NX):
            for copy in x_peer_copies(d):
                copy.start()
        st_buf[cx] = st_own[cx]
        tl_buf[cx] = tl_own[pl.ds(pl.multiple_of(cx * eight, eight), eight), :]

    def z_peer_copies(d):
        target = lax.rem(cz + d, nz)
        return (
            remote(rq, zr_buf.at[cz], s2_s.at[d], s2_r.at[d], at_z(target)),
            remote(tlr, ztl_buf.at[cz], t2_s.at[d], t2_r.at[d], at_z(target)),
        )

    def spread(shrink):
        return jnp.concatenate([pair_row(shrink, k) for k in range(qpairs)], axis=1)

    def row_state():
        for d in range(1, NX):
            for copy in x_peer_copies(d):
                copy.wait_recv()
        running = jnp.zeros((NS, quarter), F32)
        whole = jnp.zeros((eight, 128), F32)
        for x in range(NX):
            prefix[x] = running
            running = running * spread(jnp.exp(tl_buf[x])) + st_buf[x].astype(F32)
            whole = whole + tl_buf[x]
        rq[...] = running.astype(BF16)
        tlr[...] = whole
        for d in range(1, nz):

            @pl.when(cz + d < nz)
            def _(d=d):
                for copy in z_peer_copies(d):
                    copy.start()

    columns_of = lambda x: pl.ds(pl.multiple_of(x * quarter, quarter), quarter)

    def ent_copy(d):
        peer = lax.rem(cx + d, NX)
        return remote(
            ent_own.at[peer], ent.at[:, columns_of(cx)], s3_s.at[d], s3_r.at[d], at_x(peer)
        )

    def ent_arrival(d):
        peer = lax.rem(cx + NX - d, NX)
        return remote(
            ent_own.at[peer], ent.at[:, columns_of(peer)], s3_s.at[d], s3_r.at[d], at_x(peer)
        )

    def entering_rows():
        eq[...] = jnp.zeros_like(eq)
        for d in range(1, nz):

            @pl.when(cz >= d)
            def _(d=d):
                for copy in z_peer_copies(d):
                    copy.wait_recv()

        @pl.loop(0, cz)
        def _(z):
            eq[...] = eq[...] * spread(jnp.exp(ztl_buf[z])) + zr_buf[z].astype(F32)

        passed = eq[...]
        reach = jnp.zeros((eight, 128), F32)
        for x in range(NX):
            ent_own[x] = (passed * spread(jnp.exp(reach)) + prefix[x]).astype(BF16)
            reach = reach + tl_buf[x]
        for d in range(1, NX):
            ent_copy(d).start()
        ent[:, columns_of(cx)] = ent_own[cx]

    def finish():
        for d in range(1, NX):
            ent_arrival(d).wait_recv()
        load_z.wait()
        b_high, b_low = parts2(vector_rows(0))
        c_high, c_low = parts2(vector_rows(2))
        c3 = jnp.concatenate([c_high, c_low, c_high], axis=0)
        c2 = jnp.concatenate([c_high, c_low], axis=0)
        scores = tn(c3, jnp.concatenate([b_high, b_high, b_low], axis=0))
        first = lax.broadcasted_iota(jnp.int32, (rows, rows), 0)
        second = lax.broadcasted_iota(jnp.int32, (rows, rows), 1)
        scores = jnp.where(first >= second, scores, 0.0)
        for k in range(pairs):
            columns = slice(128 * k, 128 * k + 128)
            here = xc[:, columns]
            local_terms = []
            far_decays = []
            for h in (2 * k, 2 * k + 1):
                level = cumt_ref[:, h : h + 1]
                gap = level - cum_ref[h : h + 1, :]
                mixing = jnp.exp(jnp.minimum(gap, 0.0)) * scores * step_ref[h : h + 1, :]
                local_terms.append(nn(mixing.astype(BF16), here))
                far_decays.append(jnp.broadcast_to(jnp.exp(level), (rows, 128)))
            entering = ent[:, columns]
            carried = tn(c2, jnp.concatenate([entering, entering], axis=0))
            lane = lax.broadcasted_iota(jnp.int32, (rows, 128), 1) < PM
            gain = jnp.where(lane, skip_ref[2 * k], skip_ref[2 * k + 1])
            y = (
                jnp.where(lane, local_terms[0], local_terms[1])
                + carried * jnp.where(lane, far_decays[0], far_decays[1])
                + gain * here.astype(F32)
            )
            gate = zv[:, columns].astype(F32)
            mo[:, columns] = (y * (gate * jax.nn.sigmoid(gate))).astype(BF16)

    added_state()
    far_events(1)
    side_events(1)
    span = NX * rows

    @pl.loop(1, FORWARD + 1)
    def _(t):
        @pl.loop(0, 2)
        def _(way):
            @pl.when(way == 0)
            def _():
                own_events(t + 1)

            @pl.when(way == 1)
            def _():
                far_events(t + 1)
                side_events(t + 1)

                @pl.when(t == 1)
                def _():
                    row_state()

                @pl.when(t == 2)
                def _():
                    entering_rows()

            above, is_above = row_up(t)
            below, is_below = row_down(t)
            r = jnp.where(way == 0, above, below)
            real = ((way == 0) & is_above) | ((way == 1) & is_below & (below < cz))

            @pl.when(real)
            def _():
                attend(jnp.maximum(r, 0) * span, span, False)

    finish()
    for h in range(qheads):
        ao[:, HD * h : HD * h + HD] = (acc[h, :, :HD] / acc[h, :, HD:]).astype(BF16)

    @pl.when(ci < nctx - 1)
    def _():
        halo_copy().wait_send()

    @pl.loop(0, nz)
    def _(r):
        @pl.when(goes_up(r))
        def _():
            own_up(r).wait_send()
            far_up(r).wait_send()

        @pl.when(goes_down(r))
        def _():
            own_down(r).wait_send()
            far_down(r).wait_send()

        @pl.when(r <= cz)
        def _():
            to_right(r).wait_send()
            to_left(r).wait_send()

    for which in range(2):
        half_copy(which).wait_send()
    for d in range(1, nh):
        rs_copy(d).wait_send()
        ag_copy(d).wait_send()
    for d in range(1, NX):
        for copy in x_peer_copies(d):
            copy.wait_send()
        ent_copy(d).wait_send()
    for d in range(1, nz):

        @pl.when(cz + d < nz)
        def _(d=d):
            for copy in z_peer_copies(d):
                copy.wait_send()


def body(
    dims,
    x_in,
    z_gate,
    step_size,
    decay_rate,
    conv_weight,
    conv_bias,
    bc_proj,
    skip_gain,
    queries,
    keys,
    values,
):
    nz, nh = dims
    rows, channels = x_in.shape
    heads = step_size.shape[0]
    qheads = queries.shape[1] // HD
    span = NX * nz * rows
    quarter = channels // NX
    dma = pltpu.SemaphoreType.DMA
    vmem = pl.BlockSpec(memory_space=pltpu.VMEM)
    smem = pl.BlockSpec(memory_space=pltpu.SMEM)
    hbm = pl.BlockSpec(memory_space=pltpu.HBM)
    v = pltpu.VMEM
    scratch = [
        v((rows, channels), BF16),
        v((rows, channels), BF16),
        v((rows, qheads * HD), BF16),
        v((2, span, HD), BF16),
        v((heads, rows), F32),
        v((KW, channels), BF16),
        v((1, channels), BF16),
        v((2 * NS, channels), BF16),
        v((16, channels), BF16),
        v((16 + rows, 256), F32),
        v((rows, channels), BF16),
        v((qheads, rows, 2 * HD), BF16),
        v((qheads, rows, 128), F32),
        v((qheads, rows, 2 * HD), F32),
        v((8, 8, 128), F32),
        v((8, 8, 128), F32),
        v((8, 8, 128), F32),
        v((heads, rows), F32),
        v((heads, rows), F32),
        v((rows, heads), F32),
        v((NX, NS, quarter), BF16),
        v((heads, 128), F32),
        v((NX, NS, quarter), BF16),
        v((NX, heads // NX, 128), F32),
        v((NX, NS, quarter), F32),
        v((NS, quarter), BF16),
        v((heads // NX, 128), F32),
        v((nz, NS, quarter), BF16),
        v((nz, heads // NX, 128), F32),
        v((NS, quarter), F32),
        v((NX, NS, quarter), BF16),
        v((NS, channels), BF16),
        dma((9,)),
        dma((1,)),
        dma((1,)),
        *[dma((nz,)) for _ in range(10)],
        *[dma((2,)) for _ in range(2)],
        *[dma((nh,)) for _ in range(4)],
        *[dma((NX,)) for _ in range(4)],
        *[dma((nz,)) for _ in range(4)],
        *[dma((NX,)) for _ in range(2)],
    ]
    return pl.pallas_call(
        functools.partial(kernel, dims),
        out_shape=(
            jax.ShapeDtypeStruct((rows, channels), BF16),
            jax.ShapeDtypeStruct((rows, qheads * HD), BF16),
        ),
        in_specs=[hbm, hbm, hbm, smem, hbm, hbm, hbm, smem, hbm, hbm, hbm],
        out_specs=(vmem, vmem),
        scratch_shapes=scratch,
        compiler_params=pltpu.CompilerParams(
            collective_id=0, has_side_effects=True, vmem_limit_bytes=60 << 20
        ),
    )(
        x_in,
        z_gate,
        step_size,
        decay_rate,
        conv_weight,
        conv_bias.reshape(1, channels),
        bc_proj,
        skip_gain,
        queries,
        keys,
        values,
    )


def solution(mesh):
    dims = (mesh.shape["ctx"] // NX, mesh.shape["head"])
    return jax.shard_map(
        functools.partial(body, dims),
        mesh=mesh,
        in_specs=(
            P("ctx", "head"),
            P("ctx", "head"),
            P("head", "ctx"),
            P("head"),
            P(None, "head"),
            P("head"),
            P(None, "head"),
            P("head"),
            P("ctx", "head"),
            P("ctx", "head"),
            P("ctx", "head"),
        ),
        out_specs=(P("ctx", "head"), P("ctx", "head")),
        check_vma=False,
    )
```

```python
import functools
import jax
import jax.numpy as jnp
from jax import lax
from jax.experimental import pallas as pl
from jax.experimental.pallas import tpu as pltpu
from jax.sharding import PartitionSpec as P

NS = 16
KW = 4
HD = 128
PM = 64
BLOCK = 256
NX = 4
FORWARD = 4
MESH = pl.DeviceIdType.MESH
F32 = jnp.float32
BF16 = jnp.bfloat16
NEG = -1e30


def nt(a, b):
    return lax.dot_general(a, b, (((1,), (1,)), ((), ())), preferred_element_type=F32)


def tn(a, b):
    return lax.dot_general(a, b, (((0,), (0,)), ((), ())), preferred_element_type=F32)


def nn(a, b):
    return lax.dot_general(a, b, (((1,), (0,)), ((), ())), preferred_element_type=F32)


def parts2(a):
    high = a.astype(BF16)
    return high, (a - high.astype(F32)).astype(BF16)


def parts3(a):
    high = a.astype(BF16)
    rest = a - high.astype(F32)
    middle = rest.astype(BF16)
    return high, middle, (rest - middle.astype(F32)).astype(BF16)


def kernel(
    dims,
    x_hbm,
    z_hbm,
    step_hbm,
    rate_ref,
    taps_hbm,
    bias_hbm,
    proj_hbm,
    skip_ref,
    q_hbm,
    k_hbm,
    v_hbm,
    mo,
    ao,
    xv,
    zv,
    qv,
    kv,
    step_ref,
    taps_ref,
    bias_ref,
    bias_wide,
    proj_ref,
    halo,
    padded,
    rim,
    xc,
    qp,
    best,
    acc,
    part,
    rs_buf,
    ag_buf,
    ld,
    cum_ref,
    cumt_ref,
    st_own,
    tl_own,
    st_buf,
    tl_buf,
    prefix,
    rq,
    tlr,
    zr_buf,
    ztl_buf,
    eq,
    ent_own,
    ent,
    loc,
    halo_s,
    halo_r,
    of_s,
    ob_s,
    o_r,
    ff_s,
    fb_s,
    f_r,
    fl_s,
    fl_r,
    fr_s,
    fr_r,
    half_s,
    half_r,
    rs_s,
    rs_r,
    ag_s,
    ag_r,
    s1_s,
    s1_r,
    t1_s,
    t1_r,
    s2_s,
    s2_r,
    t2_s,
    t2_r,
    s3_s,
    s3_r,
):
    nz, nh = dims
    rows, channels = xv.shape
    heads = step_ref.shape[0]
    pairs = channels // 128
    quarter = channels // NX
    qpairs = quarter // 128
    qheads = qp.shape[0]
    ci = lax.axis_index("ctx")
    hi = lax.axis_index("head")
    cz = lax.div(ci, NX)
    cx = lax.rem(ci, NX)
    nctx = nz * NX

    def at_z(z):
        return {"ctx": z * NX + cx}

    def at_x(x):
        return {"ctx": cz * NX + x}

    def turned(x):
        return lax.rem(x + 2 * NX, NX)

    def local(src, dst, number):
        return pltpu.make_async_copy(src, dst, loc.at[number])

    own = pl.ds(pl.multiple_of(ci * rows, rows), rows)
    load_k = local(k_hbm, kv.at[0, own], 0)
    load_v = local(v_hbm, kv.at[1, own], 1)
    load_q = local(q_hbm, qv, 2)
    load_x = local(x_hbm, xv, 3)
    load_z = local(z_hbm, zv, 4)
    small = [
        local(step_hbm, step_ref, 5),
        local(taps_hbm, taps_ref, 6),
        local(bias_hbm, bias_ref, 7),
        local(proj_hbm, proj_ref, 8),
    ]
    for copy in [load_k, load_v, load_q, *small, load_x, load_z]:
        copy.start()

    barrier = pltpu.get_barrier_semaphore()

    def greet(device):
        pl.semaphore_signal(barrier, inc=1, device_id=device, device_id_type=MESH)

    for d in range(1, nh):
        greet({"head": lax.rem(hi + d, nh)})
    for d in range(1, NX):
        greet(at_x(lax.rem(cx + d, NX)))
    for d in range(1, nz):
        greet(at_z(lax.rem(cz + d, nz)))
    greet({"ctx": lax.rem(ci + 1, nctx)})
    greet({"ctx": lax.rem(ci + nctx - 1, nctx)})

    load_k.wait()
    load_v.wait()
    for copy in small:
        copy.wait()

    pl.semaphore_wait(barrier, nh + NX + nz - 1)

    def remote(src, dst, send, recv, device):
        return pltpu.make_async_remote_copy(
            src_ref=src,
            dst_ref=dst,
            send_sem=send,
            recv_sem=recv,
            device_id=device,
            device_id_type=MESH,
        )

    def halo_copy():
        return remote(
            x_hbm.at[pl.ds(rows - 16, 16)],
            halo,
            halo_s.at[0],
            halo_r.at[0],
            {"ctx": lax.rem(ci + 1, nctx)},
        )

    @pl.when(ci < nctx - 1)
    def _():
        halo_copy().start()

    def place(r, x):
        return pl.ds(pl.multiple_of((r * NX + x) * rows, rows), rows)

    def moved(r, x, send, recv, device):
        block = kv.at[:, place(r, x), :]
        return remote(block, block, send, recv, device)

    opposite = turned(cx + 2)
    up = at_z(lax.rem(cz + 1, nz))
    down = at_z(lax.rem(cz + nz - 1, nz))

    def own_up(r):
        return moved(r, cx, of_s.at[r], o_r.at[r], up)

    def own_down(r):
        return moved(r, cx, ob_s.at[r], o_r.at[r], down)

    def far_up(r):
        return moved(r, opposite, ff_s.at[r], f_r.at[r], up)

    def far_down(r):
        return moved(r, opposite, fb_s.at[r], f_r.at[r], down)

    def to_right(r):
        return moved(r, cx, fl_s.at[r], fl_r.at[r], at_x(turned(cx + 1)))

    def to_left(r):
        return moved(r, cx, fr_s.at[r], fr_r.at[r], at_x(turned(cx - 1)))

    def half_copy(which):
        source, target = ((cx - 1, cx + 1), (cx + 1, cx - 1))[which]
        block = kv.at[which, place(cz, turned(source)), :]
        return remote(
            block, block, half_s.at[which], half_r.at[which], at_x(turned(target))
        )

    def hops_down(r):
        return lax.rem(r - cz + nz, nz)

    def goes_up(r):
        return (cz < nz - 1) & (cz - r >= 0) & (cz - r < FORWARD)

    def goes_down(r):
        return (r < nz - 1 - FORWARD) & (hops_down(r) < nz - 1 - FORWARD)

    def send_own(r, sideways):
        @pl.when(goes_up(r))
        def _():
            own_up(r).start()

        @pl.when(goes_down(r))
        def _():
            own_down(r).start()

        @pl.when(sideways)
        def _():
            to_right(r).start()
            to_left(r).start()

    def send_far(r):
        @pl.when(goes_up(r))
        def _():
            far_up(r).start()

        @pl.when(goes_down(r))
        def _():
            far_down(r).start()

    def row_up(t):
        return cz - t, (cz - t >= 0) & (t <= FORWARD)

    def row_down(t):
        r = lax.rem(cz + t, nz)
        return r, (r < nz - 1 - FORWARD) & (t <= nz - 1 - FORWARD)

    def own_events(t):
        for r, real in (row_up(t), row_down(t)):

            @pl.when(real)
            def _(r=r):
                safe = jnp.maximum(r, 0)
                own_up(safe).wait_recv()
                send_own(safe, safe < cz)

    def far_events(t):
        for r, real in (row_up(t), row_down(t)):

            @pl.when(real)
            def _(r=r):
                safe = jnp.maximum(r, 0)
                far_up(safe).wait_recv()
                send_far(safe)

    def side_events(t):
        for r, real in (row_up(t), row_down(t)):

            @pl.when(real & (r < cz))
            def _(r=r):
                safe = jnp.maximum(r, 0)
                to_right(safe).wait_recv()
                to_left(safe).wait_recv()

    send_own(cz, True)

    load_x.wait()
    width = padded.shape[1]

    def column_piece(piece):
        return pl.ds(pl.multiple_of(piece * width, width), width)

    bias_wide[...] = bias_ref[...].astype(F32)

    def convolve(ext, count, piece):
        columns = column_piece(piece)
        edge = ext.shape[0] - count
        rising = jnp.concatenate(
            [bias_wide[pl.ds(piece * (width // 128) + j, 1), :] for j in range(width // 128)], axis=1
        )
        summed = jnp.broadcast_to(rising, (count, width))
        for offset in range(KW):
            low = edge - KW + 1 + offset
            summed = summed + ext[low : low + count, :] * taps_ref[
                offset : offset + 1, columns
            ].astype(F32)
        return (summed * jax.nn.sigmoid(summed)).astype(BF16)

    padded[0:16, :] = jnp.zeros((16, width), F32)

    @pl.loop(0, channels // width)
    def _(piece):
        columns = column_piece(piece)
        padded[16 : 16 + rows, :] = xv[:, columns].astype(F32)
        xc[:, columns] = convolve(padded, rows, piece)

    load_q.wait()
    factor = (HD**-0.5) * 1.4426950408889634
    for h in range(qheads):
        high, low = parts2(qv[:, HD * h : HD * h + HD].astype(F32) * factor)
        qp[h, :, :HD] = high
        qp[h, :, HD:] = low
    for h in range(heads):
        ld[h : h + 1, :] = step_ref[h : h + 1, :] * (-rate_ref[h])
    first = lax.broadcasted_iota(jnp.int32, (rows, rows), 0)
    second = lax.broadcasted_iota(jnp.int32, (rows, rows), 1)
    upper = (first <= second).astype(F32).astype(BF16)
    lower = (first >= second).astype(F32).astype(BF16)
    pieces = parts3(ld[...])
    cum = nn(pieces[0], upper) + (nn(pieces[1], upper) + nn(pieces[2], upper))
    cum_ref[...] = cum
    cumt_ref[...] = nt(lower, pieces[0]) + (nt(lower, pieces[1]) + nt(lower, pieces[2]))
    tl_own[...] = jnp.broadcast_to(cum[:, rows - 1 : rows], (heads, 128))

    eight = 2 * qpairs

    def x_log_copy(d):
        peer = lax.rem(cx + d, NX)
        its = pl.ds(pl.multiple_of(peer * eight, eight), eight)
        return remote(tl_own.at[its], tl_buf.at[cx], t1_s.at[d], t1_r.at[d], at_x(peer))

    def z_log_copy(d):
        target = lax.rem(cz + d, nz)
        return remote(tlr, ztl_buf.at[cz], t2_s.at[d], t2_r.at[d], at_z(target))

    for d in range(1, NX):
        x_log_copy(d).start()
    tl_buf[cx] = tl_own[pl.ds(pl.multiple_of(cx * eight, eight), eight), :]

    def attend(start, span, opening):
        keys = kv[0, pl.ds(pl.multiple_of(start, rows), span), :]
        values = kv[1, pl.ds(pl.multiple_of(start, rows), span), :]
        keys2 = jnp.concatenate([keys, keys], axis=1)
        values2 = jnp.concatenate([values, jnp.ones((span, HD), BF16)], axis=1)

        unroll = qheads

        @pl.loop(0, qheads // unroll)
        def _(g):
            group = [g * unroll + u for u in range(unroll)]
            for h, s in [(h, nt(qp[h], keys2)) for h in group]:
                if opening:
                    token = lax.broadcasted_iota(jnp.int32, (rows, span), 0)
                    position = lax.broadcasted_iota(jnp.int32, (rows, span), 1)
                    s = jnp.where(token >= position, s, NEG)
                top = jnp.max(s, axis=1, keepdims=True)
                if opening:
                    new = jnp.broadcast_to(top, (rows, 128))
                else:
                    old = best[h]
                    new = jnp.maximum(old, top)
                weights = jnp.concatenate(
                    [
                        jnp.exp2(s[:, 128 * j : 128 * j + 128] - new).astype(BF16)
                        for j in range(span // 128)
                    ],
                    axis=1,
                )
                product = nn(weights, values2)
                if opening:
                    acc[h] = product
                else:
                    shrink = jnp.exp2(old - new)
                    acc[h] = acc[h] * jnp.concatenate([shrink, shrink], axis=1) + product
                best[h] = new

    to_right(cz).wait_recv()
    to_left(cz).wait_recv()
    for which in range(2):
        half_copy(which).start()
    own_events(1)

    @pl.when(ci > 0)
    def _():
        halo_copy().wait_recv()

        @pl.loop(0, channels // width)
        def _(piece):
            columns = column_piece(piece)
            rim[0:16, :] = halo[:, columns].astype(F32)
            rim[16:32, :] = xv[0:16, columns].astype(F32)
            xc[0:16, columns] = convolve(rim, 16, piece)

    partial = nt(proj_ref[...], xc[...])
    for p in range(8):
        part[p] = partial[8 * (p // 2) : 8 * (p // 2) + 8, 128 * (p % 2) : 128 * (p % 2) + 128]

    def rs_copy(d):
        peer = lax.rem(hi + d, nh)
        return remote(
            part.at[peer], rs_buf.at[hi], rs_s.at[d], rs_r.at[d], {"head": peer}
        )

    def ag_copy(d):
        peer = lax.rem(hi + d, nh)
        return remote(
            ag_buf.at[hi], ag_buf.at[hi], ag_s.at[d], ag_r.at[d], {"head": peer}
        )

    for d in range(1, nh):
        rs_copy(d).start()
    rs_buf[hi] = part[hi]

    for d in range(1, NX):
        x_log_copy(d).wait_recv()
    tlr[...] = (tl_buf[0] + tl_buf[1]) + (tl_buf[2] + tl_buf[3])
    for d in range(1, nz):

        @pl.when(cz + d < nz)
        def _(d=d):
            z_log_copy(d).start()

    attend(ci * rows, rows, True)
    for d in range(1, nh):
        rs_copy(d).wait_recv()
    total = rs_buf[0]
    for p in range(1, nh):
        total = total + rs_buf[p]
    ag_buf[hi] = total
    for d in range(1, nh):
        ag_copy(d).start()

    for which in range(2):
        half_copy(which).wait_recv()
    send_far(cz)

    @pl.loop(0, cx)
    def _(x):
        attend((cz * NX + x) * rows, rows, False)

    own_events(2)
    def vector_rows(first_group):
        return jnp.concatenate(
            [
                jnp.concatenate([ag_buf[2 * g], ag_buf[2 * g + 1]], axis=1)
                for g in (first_group, first_group + 1)
            ],
            axis=0,
        )

    def lane_pick(a, b):
        lane = lax.broadcasted_iota(jnp.int32, a.shape, 1)
        return jnp.where(lane < PM, a, b)

    def pair_row(logs, k):
        return lane_pick(logs[2 * k : 2 * k + 1], logs[2 * k + 1 : 2 * k + 2])

    def x_state_copy(d):
        peer = lax.rem(cx + d, NX)
        return remote(st_own.at[peer], st_buf.at[cx], s1_s.at[d], s1_r.at[d], at_x(peer))

    def added_state():
        b_rows = vector_rows(0)
        cum = cum_ref[...]
        tail = jnp.exp(cum[:, rows - 1 : rows] - cum) * step_ref[...]
        for k in range(pairs):
            weighted = jnp.concatenate(
                [tail[2 * k : 2 * k + 1] * b_rows, tail[2 * k + 1 : 2 * k + 2] * b_rows],
                axis=0,
            )
            high, low = parts2(weighted)
            out = nn(jnp.concatenate([high, low], axis=0), xc[:, 128 * k : 128 * k + 128])
            out = out[: 2 * NS] + out[2 * NS :]
            into = slice(128 * (k % qpairs), 128 * (k % qpairs) + 128)
            st_own[k // qpairs, :, into] = lane_pick(out[:NS], out[NS:]).astype(BF16)
        for d in range(1, NX):
            x_state_copy(d).start()
        st_buf[cx] = st_own[cx]

    def z_state_copy(d):
        target = lax.rem(cz + d, nz)
        return remote(rq, zr_buf.at[cz], s2_s.at[d], s2_r.at[d], at_z(target))

    def spread(shrink):
        return jnp.concatenate([pair_row(shrink, k) for k in range(qpairs)], axis=1)

    def row_state():
        for d in range(1, NX):
            x_state_copy(d).wait_recv()
        running = jnp.zeros((NS, quarter), F32)
        for x in range(NX):
            prefix[x] = running
            running = running * spread(jnp.exp(tl_buf[x])) + st_buf[x].astype(F32)
        rq[...] = running.astype(BF16)
        for d in range(nz - 1, 0, -1):

            @pl.when(cz + d < nz)
            def _(d=d):
                z_state_copy(d).start()

    columns_of = lambda x: pl.ds(pl.multiple_of(x * quarter, quarter), quarter)

    def ent_copy(d):
        peer = lax.rem(cx + d, NX)
        return remote(
            ent_own.at[peer], ent.at[:, columns_of(cx)], s3_s.at[d], s3_r.at[d], at_x(peer)
        )

    def ent_arrival(d):
        peer = lax.rem(cx + NX - d, NX)
        return remote(
            ent_own.at[peer], ent.at[:, columns_of(peer)], s3_s.at[d], s3_r.at[d], at_x(peer)
        )

    def entering_rows():
        eq[...] = jnp.zeros_like(eq)
        for d in range(1, nz):

            @pl.when(cz >= d)
            def _(d=d):
                z_state_copy(d).wait_recv()
                z_log_copy(d).wait_recv()

        @pl.loop(0, cz)
        def _(z):
            eq[...] = eq[...] * spread(jnp.exp(ztl_buf[z])) + zr_buf[z].astype(F32)

        passed = eq[...]
        reach = jnp.zeros((eight, 128), F32)
        for x in range(NX):
            ent_own[x] = (passed * spread(jnp.exp(reach)) + prefix[x]).astype(BF16)
            reach = reach + tl_buf[x]
        for d in range(1, NX):
            ent_copy(d).start()
        ent[:, columns_of(cx)] = ent_own[cx]

    def finish():
        for d in range(1, NX):
            ent_arrival(d).wait_recv()
        load_z.wait()
        b_high, b_low = parts2(vector_rows(0))
        c_high, c_low = parts2(vector_rows(2))
        c3 = jnp.concatenate([c_high, c_low, c_high], axis=0)
        c2 = jnp.concatenate([c_high, c_low], axis=0)
        scores = tn(c3, jnp.concatenate([b_high, b_high, b_low], axis=0))
        first = lax.broadcasted_iota(jnp.int32, (rows, rows), 0)
        second = lax.broadcasted_iota(jnp.int32, (rows, rows), 1)
        scores = jnp.where(first >= second, scores, 0.0)
        for k in range(pairs):
            columns = slice(128 * k, 128 * k + 128)
            here = xc[:, columns]
            local_terms = []
            far_decays = []
            for h in (2 * k, 2 * k + 1):
                level = cumt_ref[:, h : h + 1]
                gap = level - cum_ref[h : h + 1, :]
                mixing = jnp.exp(jnp.minimum(gap, 0.0)) * scores * step_ref[h : h + 1, :]
                local_terms.append(nn(mixing.astype(BF16), here))
                far_decays.append(jnp.broadcast_to(jnp.exp(level), (rows, 128)))
            entering = ent[:, columns]
            carried = tn(c2, jnp.concatenate([entering, entering], axis=0))
            lane = lax.broadcasted_iota(jnp.int32, (rows, 128), 1) < PM
            gain = jnp.where(lane, skip_ref[2 * k], skip_ref[2 * k + 1])
            y = (
                jnp.where(lane, local_terms[0], local_terms[1])
                + carried * jnp.where(lane, far_decays[0], far_decays[1])
                + gain * here.astype(F32)
            )
            gate = zv[:, columns].astype(F32)
            mo[:, columns] = (y * (gate * jax.nn.sigmoid(gate))).astype(BF16)

    for d in range(1, nh):
        ag_copy(d).wait_recv()
    added_state()
    span = NX * rows

    @pl.loop(0, 2 * FORWARD - 1)
    def _(u):
        @pl.when(u == 0)
        def _():
            far_events(1)
            side_events(1)

        @pl.when(u == 1)
        def _():
            row_state()
            own_events(3)
            far_events(2)
            side_events(2)

        @pl.when(u == 2)
        def _():
            own_events(4)

        @pl.when(u == 3)
        def _():
            far_events(3)
            side_events(3)
            entering_rows()

        @pl.when(u == 5)
        def _():
            far_events(4)
            side_events(4)

        t = lax.div(u, 2) + 1
        way = lax.rem(u, 2)
        above, is_above = row_up(t)
        below, is_below = row_down(t)
        r = jnp.where(way == 0, above, below)
        real = ((way == 0) & is_above) | ((way == 1) & is_below & (below < cz))

        @pl.when(real)
        def _():
            attend(jnp.maximum(r, 0) * span, span, False)

    finish()
    for h in range(qheads):
        ao[:, HD * h : HD * h + HD] = (acc[h, :, :HD] / acc[h, :, HD:]).astype(BF16)

    @pl.when(ci < nctx - 1)
    def _():
        halo_copy().wait_send()

    @pl.loop(0, nz)
    def _(r):
        @pl.when(goes_up(r))
        def _():
            own_up(r).wait_send()
            far_up(r).wait_send()

        @pl.when(goes_down(r))
        def _():
            own_down(r).wait_send()
            far_down(r).wait_send()

        @pl.when(r <= cz)
        def _():
            to_right(r).wait_send()
            to_left(r).wait_send()

    for which in range(2):
        half_copy(which).wait_send()
    for d in range(1, nh):
        rs_copy(d).wait_send()
        ag_copy(d).wait_send()
    for d in range(1, NX):
        x_state_copy(d).wait_send()
        x_log_copy(d).wait_send()
        ent_copy(d).wait_send()
    for d in range(1, nz):

        @pl.when(cz + d < nz)
        def _(d=d):
            z_state_copy(d).wait_send()
            z_log_copy(d).wait_send()


def body(
    dims,
    x_in,
    z_gate,
    step_size,
    decay_rate,
    conv_weight,
    conv_bias,
    bc_proj,
    skip_gain,
    queries,
    keys,
    values,
):
    nz, nh = dims
    rows, channels = x_in.shape
    heads = step_size.shape[0]
    qheads = queries.shape[1] // HD
    span = NX * nz * rows
    quarter = channels // NX
    dma = pltpu.SemaphoreType.DMA
    vmem = pl.BlockSpec(memory_space=pltpu.VMEM)
    smem = pl.BlockSpec(memory_space=pltpu.SMEM)
    hbm = pl.BlockSpec(memory_space=pltpu.HBM)
    v = pltpu.VMEM
    scratch = [
        v((rows, channels), BF16),
        v((rows, channels), BF16),
        v((rows, qheads * HD), BF16),
        v((2, span, HD), BF16),
        v((heads, rows), F32),
        v((KW, channels), BF16),
        v((channels // 128, 128), BF16),
        v((channels // 128, 128), F32),
        v((2 * NS, channels), BF16),
        v((16, channels), BF16),
        v((16 + rows, 256), F32),
        v((32, 256), F32),
        v((rows, channels), BF16),
        v((qheads, rows, 2 * HD), BF16),
        v((qheads, rows, 128), F32),
        v((qheads, rows, 2 * HD), F32),
        v((8, 8, 128), F32),
        v((8, 8, 128), F32),
        v((8, 8, 128), F32),
        v((heads, rows), F32),
        v((heads, rows), F32),
        v((rows, heads), F32),
        v((NX, NS, quarter), BF16),
        v((heads, 128), F32),
        v((NX, NS, quarter), BF16),
        v((NX, heads // NX, 128), F32),
        v((NX, NS, quarter), F32),
        v((NS, quarter), BF16),
        v((heads // NX, 128), F32),
        v((nz, NS, quarter), BF16),
        v((nz, heads // NX, 128), F32),
        v((NS, quarter), F32),
        v((NX, NS, quarter), BF16),
        v((NS, channels), BF16),
        dma((9,)),
        dma((1,)),
        dma((1,)),
        *[dma((nz,)) for _ in range(10)],
        *[dma((2,)) for _ in range(2)],
        *[dma((nh,)) for _ in range(4)],
        *[dma((NX,)) for _ in range(4)],
        *[dma((nz,)) for _ in range(4)],
        *[dma((NX,)) for _ in range(2)],
    ]
    return pl.pallas_call(
        functools.partial(kernel, dims),
        out_shape=(
            jax.ShapeDtypeStruct((rows, channels), BF16),
            jax.ShapeDtypeStruct((rows, qheads * HD), BF16),
        ),
        in_specs=[hbm, hbm, hbm, smem, hbm, hbm, hbm, smem, hbm, hbm, hbm],
        out_specs=(vmem, vmem),
        scratch_shapes=scratch,
        compiler_params=pltpu.CompilerParams(
            collective_id=0, has_side_effects=True, vmem_limit_bytes=60 << 20
        ),
    )(
        x_in,
        z_gate,
        step_size,
        decay_rate,
        conv_weight,
        conv_bias.reshape(channels // 128, 128),
        bc_proj,
        skip_gain,
        queries,
        keys,
        values,
    )


def solution(mesh):
    dims = (mesh.shape["ctx"] // NX, mesh.shape["head"])
    return jax.shard_map(
        functools.partial(body, dims),
        mesh=mesh,
        in_specs=(
            P("ctx", "head"),
            P("ctx", "head"),
            P("head", "ctx"),
            P("head"),
            P(None, "head"),
            P("head"),
            P(None, "head"),
            P("head"),
            P("ctx", "head"),
            P("ctx", "head"),
            P("ctx", "head"),
        ),
        out_specs=(P("ctx", "head"), P("ctx", "head")),
        check_vma=False,
    )
```

```python
import functools
import jax
import jax.numpy as jnp
from jax import lax
from jax.experimental import pallas as pl
from jax.experimental.pallas import tpu as pltpu
from jax.sharding import PartitionSpec as P

NS = 16
KW = 4
HD = 128
PM = 64
BLOCK = 256
NX = 4
FORWARD = 4
MESH = pl.DeviceIdType.MESH
F32 = jnp.float32
BF16 = jnp.bfloat16
NEG = -1e30


def nt(a, b):
    return lax.dot_general(a, b, (((1,), (1,)), ((), ())), preferred_element_type=F32)


def tn(a, b):
    return lax.dot_general(a, b, (((0,), (0,)), ((), ())), preferred_element_type=F32)


def nn(a, b):
    return lax.dot_general(a, b, (((1,), (0,)), ((), ())), preferred_element_type=F32)


def parts2(a):
    high = a.astype(BF16)
    return high, (a - high.astype(F32)).astype(BF16)


def parts3(a):
    high = a.astype(BF16)
    rest = a - high.astype(F32)
    middle = rest.astype(BF16)
    return high, middle, (rest - middle.astype(F32)).astype(BF16)


def kernel(
    dims,
    x_hbm,
    z_hbm,
    step_hbm,
    rate_ref,
    taps_hbm,
    bias_hbm,
    proj_hbm,
    skip_ref,
    q_hbm,
    k_hbm,
    v_hbm,
    mo,
    ao,
    xv,
    zv,
    qv,
    kv,
    step_ref,
    taps_ref,
    bias_ref,
    bias_wide,
    proj_ref,
    halo,
    padded,
    rim,
    xc,
    ybuf,
    qp,
    best,
    acc,
    part,
    rs_buf,
    ag_buf,
    ld,
    cum_ref,
    cumt_ref,
    st_own,
    tl_own,
    st_buf,
    tl_buf,
    prefix,
    rq,
    tlr,
    zr_buf,
    ztl_buf,
    eq,
    ent_own,
    ent,
    loc,
    halo_s,
    halo_r,
    of_s,
    ob_s,
    o_r,
    ff_s,
    fb_s,
    f_r,
    fl_s,
    fl_r,
    fr_s,
    fr_r,
    half_s,
    half_r,
    rs_s,
    rs_r,
    ag_s,
    ag_r,
    s1_s,
    s1_r,
    t1_s,
    t1_r,
    s2_s,
    s2_r,
    t2_s,
    t2_r,
    s3_s,
    s3_r,
):
    nz, nh = dims
    rows, channels = xv.shape
    heads = step_ref.shape[0]
    pairs = channels // 128
    quarter = channels // NX
    qpairs = quarter // 128
    qheads = qp.shape[0]
    ci = lax.axis_index("ctx")
    hi = lax.axis_index("head")
    cz = lax.div(ci, NX)
    cx = lax.rem(ci, NX)
    nctx = nz * NX

    def at_z(z):
        return {"ctx": z * NX + cx}

    def at_x(x):
        return {"ctx": cz * NX + x}

    def turned(x):
        return lax.rem(x + 2 * NX, NX)

    def local(src, dst, number):
        return pltpu.make_async_copy(src, dst, loc.at[number])

    own = pl.ds(pl.multiple_of(ci * rows, rows), rows)
    load_k = local(k_hbm, kv.at[0, own], 0)
    load_v = local(v_hbm, kv.at[1, own], 1)
    load_q = local(q_hbm, qv, 2)
    load_x = local(x_hbm, xv, 3)
    load_z = local(z_hbm, zv, 4)
    small = [
        local(step_hbm, step_ref, 5),
        local(taps_hbm, taps_ref, 6),
        local(bias_hbm, bias_ref, 7),
        local(proj_hbm, proj_ref, 8),
    ]
    for copy in [load_k, load_v, load_q, *small, load_x, load_z]:
        copy.start()

    barrier = pltpu.get_barrier_semaphore()

    def greet(device):
        pl.semaphore_signal(barrier, inc=1, device_id=device, device_id_type=MESH)

    for d in range(1, nh):
        greet({"head": lax.rem(hi + d, nh)})
    for d in range(1, NX):
        greet(at_x(lax.rem(cx + d, NX)))
    for d in range(1, nz):
        greet(at_z(lax.rem(cz + d, nz)))
    greet({"ctx": lax.rem(ci + 1, nctx)})
    greet({"ctx": lax.rem(ci + nctx - 1, nctx)})

    load_k.wait()
    load_v.wait()
    for copy in small:
        copy.wait()

    pl.semaphore_wait(barrier, nh + NX + nz - 1)

    def remote(src, dst, send, recv, device):
        return pltpu.make_async_remote_copy(
            src_ref=src,
            dst_ref=dst,
            send_sem=send,
            recv_sem=recv,
            device_id=device,
            device_id_type=MESH,
        )

    def halo_copy():
        return remote(
            x_hbm.at[pl.ds(rows - 16, 16)],
            halo,
            halo_s.at[0],
            halo_r.at[0],
            {"ctx": lax.rem(ci + 1, nctx)},
        )

    @pl.when(ci < nctx - 1)
    def _():
        halo_copy().start()

    def place(r, x):
        return pl.ds(pl.multiple_of((r * NX + x) * rows, rows), rows)

    def moved(r, x, send, recv, device):
        block = kv.at[:, place(r, x), :]
        return remote(block, block, send, recv, device)

    opposite = turned(cx + 2)
    up = at_z(lax.rem(cz + 1, nz))
    down = at_z(lax.rem(cz + nz - 1, nz))

    def own_up(r):
        return moved(r, cx, of_s.at[r], o_r.at[r], up)

    def own_down(r):
        return moved(r, cx, ob_s.at[r], o_r.at[r], down)

    def far_up(r):
        return moved(r, opposite, ff_s.at[r], f_r.at[r], up)

    def far_down(r):
        return moved(r, opposite, fb_s.at[r], f_r.at[r], down)

    def to_right(r):
        return moved(r, cx, fl_s.at[r], fl_r.at[r], at_x(turned(cx + 1)))

    def to_left(r):
        return moved(r, cx, fr_s.at[r], fr_r.at[r], at_x(turned(cx - 1)))

    def half_copy(which):
        source, target = ((cx - 1, cx + 1), (cx + 1, cx - 1))[which]
        block = kv.at[which, place(cz, turned(source)), :]
        return remote(
            block, block, half_s.at[which], half_r.at[which], at_x(turned(target))
        )

    def hops_down(r):
        return lax.rem(r - cz + nz, nz)

    def goes_up(r):
        return (cz < nz - 1) & (cz - r >= 0) & (cz - r < FORWARD)

    def goes_down(r):
        return (r < nz - 1 - FORWARD) & (hops_down(r) < nz - 1 - FORWARD)

    def send_own(r, sideways):
        @pl.when(goes_up(r))
        def _():
            own_up(r).start()

        @pl.when(goes_down(r))
        def _():
            own_down(r).start()

        @pl.when(sideways)
        def _():
            to_right(r).start()
            to_left(r).start()

    def send_far(r):
        @pl.when(goes_up(r))
        def _():
            far_up(r).start()

        @pl.when(goes_down(r))
        def _():
            far_down(r).start()

    def row_up(t):
        return cz - t, (cz - t >= 0) & (t <= FORWARD)

    def row_down(t):
        r = lax.rem(cz + t, nz)
        return r, (r < nz - 1 - FORWARD) & (t <= nz - 1 - FORWARD)

    def own_events(t):
        for r, real in (row_up(t), row_down(t)):

            @pl.when(real)
            def _(r=r):
                safe = jnp.maximum(r, 0)
                own_up(safe).wait_recv()
                send_own(safe, safe < cz)

    def far_events(t):
        for r, real in (row_up(t), row_down(t)):

            @pl.when(real)
            def _(r=r):
                safe = jnp.maximum(r, 0)
                far_up(safe).wait_recv()
                send_far(safe)

    def side_events(t):
        for r, real in (row_up(t), row_down(t)):

            @pl.when(real & (r < cz))
            def _(r=r):
                safe = jnp.maximum(r, 0)
                to_right(safe).wait_recv()
                to_left(safe).wait_recv()

    send_own(cz, True)

    load_x.wait()
    width = padded.shape[1]

    def column_piece(piece):
        return pl.ds(pl.multiple_of(piece * width, width), width)

    bias_wide[...] = bias_ref[...].astype(F32)

    def convolve(ext, count, piece):
        columns = column_piece(piece)
        edge = ext.shape[0] - count
        rising = jnp.concatenate(
            [bias_wide[pl.ds(piece * (width // 128) + j, 1), :] for j in range(width // 128)], axis=1
        )
        summed = jnp.broadcast_to(rising, (count, width))
        for offset in range(KW):
            low = edge - KW + 1 + offset
            summed = summed + ext[low : low + count, :] * taps_ref[
                offset : offset + 1, columns
            ].astype(F32)
        return (summed * jax.nn.sigmoid(summed)).astype(BF16)

    padded[0:16, :] = jnp.zeros((16, width), F32)

    @pl.loop(0, channels // width)
    def _(piece):
        columns = column_piece(piece)
        padded[16 : 16 + rows, :] = xv[:, columns].astype(F32)
        xc[:, columns] = convolve(padded, rows, piece)

    load_q.wait()
    factor = (HD**-0.5) * 1.4426950408889634
    for h in range(qheads):
        high, low = parts2(qv[:, HD * h : HD * h + HD].astype(F32) * factor)
        qp[h, :, :HD] = high
        qp[h, :, HD:] = low
    for h in range(heads):
        ld[h : h + 1, :] = step_ref[h : h + 1, :] * (-rate_ref[h])
    first = lax.broadcasted_iota(jnp.int32, (rows, rows), 0)
    second = lax.broadcasted_iota(jnp.int32, (rows, rows), 1)
    upper = (first <= second).astype(F32).astype(BF16)
    lower = (first >= second).astype(F32).astype(BF16)
    pieces = parts3(ld[...])
    cum = nn(pieces[0], upper) + (nn(pieces[1], upper) + nn(pieces[2], upper))
    cum_ref[...] = cum
    cumt_ref[...] = nt(lower, pieces[0]) + (nt(lower, pieces[1]) + nt(lower, pieces[2]))
    tl_own[...] = jnp.broadcast_to(cum[:, rows - 1 : rows], (heads, 128))

    eight = 2 * qpairs

    def x_log_copy(d):
        peer = lax.rem(cx + d, NX)
        its = pl.ds(pl.multiple_of(peer * eight, eight), eight)
        return remote(tl_own.at[its], tl_buf.at[cx], t1_s.at[d], t1_r.at[d], at_x(peer))

    def z_log_copy(d):
        target = lax.rem(cz + d, nz)
        return remote(tlr, ztl_buf.at[cz], t2_s.at[d], t2_r.at[d], at_z(target))

    for d in range(1, NX):
        x_log_copy(d).start()
    tl_buf[cx] = tl_own[pl.ds(pl.multiple_of(cx * eight, eight), eight), :]

    def attend(start, span, opening):
        keys = kv[0, pl.ds(pl.multiple_of(start, rows), span), :]
        values = kv[1, pl.ds(pl.multiple_of(start, rows), span), :]
        keys2 = jnp.concatenate([keys, keys], axis=1)
        values2 = jnp.concatenate([values, jnp.ones((span, HD), BF16)], axis=1)

        unroll = qheads

        @pl.loop(0, qheads // unroll)
        def _(g):
            group = [g * unroll + u for u in range(unroll)]
            for h, s in [(h, nt(qp[h], keys2)) for h in group]:
                if opening:
                    token = lax.broadcasted_iota(jnp.int32, (rows, span), 0)
                    position = lax.broadcasted_iota(jnp.int32, (rows, span), 1)
                    s = jnp.where(token >= position, s, NEG)
                top = jnp.max(s, axis=1, keepdims=True)
                if opening:
                    new = jnp.broadcast_to(top, (rows, 128))
                else:
                    old = best[h]
                    new = jnp.maximum(old, top)
                weights = jnp.concatenate(
                    [
                        jnp.exp2(s[:, 128 * j : 128 * j + 128] - new).astype(BF16)
                        for j in range(span // 128)
                    ],
                    axis=1,
                )
                product = nn(weights, values2)
                if opening:
                    acc[h] = product
                else:
                    shrink = jnp.exp2(old - new)
                    acc[h] = acc[h] * jnp.concatenate([shrink, shrink], axis=1) + product
                best[h] = new

    to_right(cz).wait_recv()
    to_left(cz).wait_recv()
    for which in range(2):
        half_copy(which).start()
    own_events(1)

    @pl.when(ci > 0)
    def _():
        halo_copy().wait_recv()

        @pl.loop(0, channels // width)
        def _(piece):
            columns = column_piece(piece)
            rim[0:16, :] = halo[:, columns].astype(F32)
            rim[16:32, :] = xv[0:16, columns].astype(F32)
            xc[0:16, columns] = convolve(rim, 16, piece)

    partial = nt(proj_ref[...], xc[...])
    for p in range(8):
        part[p] = partial[8 * (p // 2) : 8 * (p // 2) + 8, 128 * (p % 2) : 128 * (p % 2) + 128]

    def rs_copy(d):
        peer = lax.rem(hi + d, nh)
        return remote(
            part.at[peer], rs_buf.at[hi], rs_s.at[d], rs_r.at[d], {"head": peer}
        )

    def ag_copy(d):
        peer = lax.rem(hi + d, nh)
        return remote(
            ag_buf.at[hi], ag_buf.at[hi], ag_s.at[d], ag_r.at[d], {"head": peer}
        )

    for d in range(1, nh):
        rs_copy(d).start()
    rs_buf[hi] = part[hi]

    for d in range(1, NX):
        x_log_copy(d).wait_recv()
    tlr[...] = (tl_buf[0] + tl_buf[1]) + (tl_buf[2] + tl_buf[3])
    for d in range(1, nz):

        @pl.when(cz + d < nz)
        def _(d=d):
            z_log_copy(d).start()

    attend(ci * rows, rows, True)
    for d in range(1, nh):
        rs_copy(d).wait_recv()
    total = rs_buf[0]
    for p in range(1, nh):
        total = total + rs_buf[p]
    ag_buf[hi] = total
    for d in range(1, nh):
        ag_copy(d).start()

    for which in range(2):
        half_copy(which).wait_recv()
    send_far(cz)

    @pl.loop(0, cx)
    def _(x):
        attend((cz * NX + x) * rows, rows, False)

    own_events(2)
    def vector_rows(first_group):
        return jnp.concatenate(
            [
                jnp.concatenate([ag_buf[2 * g], ag_buf[2 * g + 1]], axis=1)
                for g in (first_group, first_group + 1)
            ],
            axis=0,
        )

    def lane_pick(a, b):
        lane = lax.broadcasted_iota(jnp.int32, a.shape, 1)
        return jnp.where(lane < PM, a, b)

    def pair_row(logs, k):
        return lane_pick(logs[2 * k : 2 * k + 1], logs[2 * k + 1 : 2 * k + 2])

    def x_state_copy(d):
        peer = lax.rem(cx + d, NX)
        return remote(st_own.at[peer], st_buf.at[cx], s1_s.at[d], s1_r.at[d], at_x(peer))

    def added_state():
        b_rows = vector_rows(0)
        cum = cum_ref[...]
        tail = jnp.exp(cum[:, rows - 1 : rows] - cum) * step_ref[...]
        for k in range(pairs):
            weighted = jnp.concatenate(
                [tail[2 * k : 2 * k + 1] * b_rows, tail[2 * k + 1 : 2 * k + 2] * b_rows],
                axis=0,
            )
            high, low = parts2(weighted)
            out = nn(jnp.concatenate([high, low], axis=0), xc[:, 128 * k : 128 * k + 128])
            out = out[: 2 * NS] + out[2 * NS :]
            into = slice(128 * (k % qpairs), 128 * (k % qpairs) + 128)
            st_own[k // qpairs, :, into] = lane_pick(out[:NS], out[NS:]).astype(BF16)
        for d in range(1, NX):
            x_state_copy(d).start()
        st_buf[cx] = st_own[cx]

    def z_state_copy(d):
        target = lax.rem(cz + d, nz)
        return remote(rq, zr_buf.at[cz], s2_s.at[d], s2_r.at[d], at_z(target))

    def spread(shrink):
        return jnp.concatenate([pair_row(shrink, k) for k in range(qpairs)], axis=1)

    def row_state():
        for d in range(1, NX):
            x_state_copy(d).wait_recv()
        running = jnp.zeros((NS, quarter), F32)
        for x in range(NX):
            prefix[x] = running
            running = running * spread(jnp.exp(tl_buf[x])) + st_buf[x].astype(F32)
        rq[...] = running.astype(BF16)
        for d in range(nz - 1, 0, -1):

            @pl.when(cz + d < nz)
            def _(d=d):
                z_state_copy(d).start()

    columns_of = lambda x: pl.ds(pl.multiple_of(x * quarter, quarter), quarter)

    def ent_copy(d):
        peer = lax.rem(cx + d, NX)
        return remote(
            ent_own.at[peer], ent.at[:, columns_of(cx)], s3_s.at[d], s3_r.at[d], at_x(peer)
        )

    def ent_arrival(d):
        peer = lax.rem(cx + NX - d, NX)
        return remote(
            ent_own.at[peer], ent.at[:, columns_of(peer)], s3_s.at[d], s3_r.at[d], at_x(peer)
        )

    def entering_rows():
        eq[...] = jnp.zeros_like(eq)
        for d in range(1, nz):

            @pl.when(cz >= d)
            def _(d=d):
                z_state_copy(d).wait_recv()
                z_log_copy(d).wait_recv()

        @pl.loop(0, cz)
        def _(z):
            eq[...] = eq[...] * spread(jnp.exp(ztl_buf[z])) + zr_buf[z].astype(F32)

        passed = eq[...]
        reach = jnp.zeros((eight, 128), F32)
        for x in range(NX):
            ent_own[x] = (passed * spread(jnp.exp(reach)) + prefix[x]).astype(BF16)
            reach = reach + tl_buf[x]
        for d in range(1, NX):
            ent_copy(d).start()
        ent[:, columns_of(cx)] = ent_own[cx]

    def within_block():
        b_high, b_low = parts2(vector_rows(0))
        c_high, c_low = parts2(vector_rows(2))
        scores = tn(
            jnp.concatenate([c_high, c_low, c_high], axis=0),
            jnp.concatenate([b_high, b_high, b_low], axis=0),
        )
        first = lax.broadcasted_iota(jnp.int32, (rows, rows), 0)
        second = lax.broadcasted_iota(jnp.int32, (rows, rows), 1)
        scores = jnp.where(first >= second, scores, 0.0)
        for k in range(pairs):
            columns = slice(128 * k, 128 * k + 128)
            here = xc[:, columns]
            local_terms = []
            for h in (2 * k, 2 * k + 1):
                gap = cumt_ref[:, h : h + 1] - cum_ref[h : h + 1, :]
                mixing = jnp.exp(jnp.minimum(gap, 0.0)) * scores * step_ref[h : h + 1, :]
                local_terms.append(nn(mixing.astype(BF16), here))
            lane = lax.broadcasted_iota(jnp.int32, (rows, 128), 1) < PM
            gain = jnp.where(lane, skip_ref[2 * k], skip_ref[2 * k + 1])
            ybuf[:, columns] = (
                jnp.where(lane, local_terms[0], local_terms[1]) + gain * here.astype(F32)
            )

    def finish():
        for d in range(1, NX):
            ent_arrival(d).wait_recv()
        load_z.wait()
        c_high, c_low = parts2(vector_rows(2))
        c2 = jnp.concatenate([c_high, c_low], axis=0)
        lane = lax.broadcasted_iota(jnp.int32, (rows, 128), 1) < PM
        for k in range(pairs):
            columns = slice(128 * k, 128 * k + 128)
            entering = ent[:, columns]
            carried = tn(c2, jnp.concatenate([entering, entering], axis=0))
            levels = jnp.where(
                lane, cumt_ref[:, 2 * k : 2 * k + 1], cumt_ref[:, 2 * k + 1 : 2 * k + 2]
            )
            y = ybuf[:, columns] + carried * jnp.exp(levels)
            gate = zv[:, columns].astype(F32)
            mo[:, columns] = (y * (gate * jax.nn.sigmoid(gate))).astype(BF16)

    for d in range(1, nh):
        ag_copy(d).wait_recv()
    added_state()
    span = NX * rows

    @pl.loop(0, 2 * FORWARD - 1)
    def _(u):
        @pl.when(u == 0)
        def _():
            far_events(1)
            side_events(1)

        @pl.when(u == 1)
        def _():
            row_state()
            own_events(3)
            within_block()
            far_events(2)
            side_events(2)

        @pl.when(u == 2)
        def _():
            own_events(4)
            entering_rows()

        @pl.when(u == 3)
        def _():
            far_events(3)
            side_events(3)

        @pl.when(u == 5)
        def _():
            far_events(4)
            side_events(4)

        t = lax.div(u, 2) + 1
        way = lax.rem(u, 2)
        above, is_above = row_up(t)
        below, is_below = row_down(t)
        r = jnp.where(way == 0, above, below)
        real = ((way == 0) & is_above) | ((way == 1) & is_below & (below < cz))

        @pl.when(real)
        def _():
            attend(jnp.maximum(r, 0) * span, span, False)

    finish()
    for h in range(qheads):
        ao[:, HD * h : HD * h + HD] = (acc[h, :, :HD] / acc[h, :, HD:]).astype(BF16)

    @pl.when(ci < nctx - 1)
    def _():
        halo_copy().wait_send()

    @pl.loop(0, nz)
    def _(r):
        @pl.when(goes_up(r))
        def _():
            own_up(r).wait_send()
            far_up(r).wait_send()

        @pl.when(goes_down(r))
        def _():
            own_down(r).wait_send()
            far_down(r).wait_send()

        @pl.when(r <= cz)
        def _():
            to_right(r).wait_send()
            to_left(r).wait_send()

    for which in range(2):
        half_copy(which).wait_send()
    for d in range(1, nh):
        rs_copy(d).wait_send()
        ag_copy(d).wait_send()
    for d in range(1, NX):
        x_state_copy(d).wait_send()
        x_log_copy(d).wait_send()
        ent_copy(d).wait_send()
    for d in range(1, nz):

        @pl.when(cz + d < nz)
        def _(d=d):
            z_state_copy(d).wait_send()
            z_log_copy(d).wait_send()


def body(
    dims,
    x_in,
    z_gate,
    step_size,
    decay_rate,
    conv_weight,
    conv_bias,
    bc_proj,
    skip_gain,
    queries,
    keys,
    values,
):
    nz, nh = dims
    rows, channels = x_in.shape
    heads = step_size.shape[0]
    qheads = queries.shape[1] // HD
    span = NX * nz * rows
    quarter = channels // NX
    dma = pltpu.SemaphoreType.DMA
    vmem = pl.BlockSpec(memory_space=pltpu.VMEM)
    smem = pl.BlockSpec(memory_space=pltpu.SMEM)
    hbm = pl.BlockSpec(memory_space=pltpu.HBM)
    v = pltpu.VMEM
    scratch = [
        v((rows, channels), BF16),
        v((rows, channels), BF16),
        v((rows, qheads * HD), BF16),
        v((2, span, HD), BF16),
        v((heads, rows), F32),
        v((KW, channels), BF16),
        v((channels // 128, 128), BF16),
        v((channels // 128, 128), F32),
        v((2 * NS, channels), BF16),
        v((16, channels), BF16),
        v((16 + rows, 256), F32),
        v((32, 256), F32),
        v((rows, channels), BF16),
        v((rows, channels), F32),
        v((qheads, rows, 2 * HD), BF16),
        v((qheads, rows, 128), F32),
        v((qheads, rows, 2 * HD), F32),
        v((8, 8, 128), F32),
        v((8, 8, 128), F32),
        v((8, 8, 128), F32),
        v((heads, rows), F32),
        v((heads, rows), F32),
        v((rows, heads), F32),
        v((NX, NS, quarter), BF16),
        v((heads, 128), F32),
        v((NX, NS, quarter), BF16),
        v((NX, heads // NX, 128), F32),
        v((NX, NS, quarter), F32),
        v((NS, quarter), BF16),
        v((heads // NX, 128), F32),
        v((nz, NS, quarter), BF16),
        v((nz, heads // NX, 128), F32),
        v((NS, quarter), F32),
        v((NX, NS, quarter), BF16),
        v((NS, channels), BF16),
        dma((9,)),
        dma((1,)),
        dma((1,)),
        *[dma((nz,)) for _ in range(10)],
        *[dma((2,)) for _ in range(2)],
        *[dma((nh,)) for _ in range(4)],
        *[dma((NX,)) for _ in range(4)],
        *[dma((nz,)) for _ in range(4)],
        *[dma((NX,)) for _ in range(2)],
    ]
    return pl.pallas_call(
        functools.partial(kernel, dims),
        out_shape=(
            jax.ShapeDtypeStruct((rows, channels), BF16),
            jax.ShapeDtypeStruct((rows, qheads * HD), BF16),
        ),
        in_specs=[hbm, hbm, hbm, smem, hbm, hbm, hbm, smem, hbm, hbm, hbm],
        out_specs=(vmem, vmem),
        scratch_shapes=scratch,
        compiler_params=pltpu.CompilerParams(
            collective_id=0, has_side_effects=True, vmem_limit_bytes=60 << 20
        ),
    )(
        x_in,
        z_gate,
        step_size,
        decay_rate,
        conv_weight,
        conv_bias.reshape(channels // 128, 128),
        bc_proj,
        skip_gain,
        queries,
        keys,
        values,
    )


def solution(mesh):
    dims = (mesh.shape["ctx"] // NX, mesh.shape["head"])
    return jax.shard_map(
        functools.partial(body, dims),
        mesh=mesh,
        in_specs=(
            P("ctx", "head"),
            P("ctx", "head"),
            P("head", "ctx"),
            P("head"),
            P(None, "head"),
            P("head"),
            P(None, "head"),
            P("head"),
            P("ctx", "head"),
            P("ctx", "head"),
            P("ctx", "head"),
        ),
        out_specs=(P("ctx", "head"), P("ctx", "head")),
        check_vma=False,
    )
```
